32 devices in a mesh: dp: 4 (over x, core), seq: 8 (over z, y).
Axes of the slice: x: 2, y: 2, z: 4, core: 2. Of those that a mesh axis runs over, the one named last changes fastest.
Arguments:
- patches: bfloat16 [4, 4096, 6144], P('dp', 'seq'), may hold values from -6 to 6
- embedding: bfloat16 [6144, 768], P('seq'), may hold values from -0.078125 to 0.078125
- first_gain: bfloat16 [768], P('seq'), may hold values from 0.5 to 1.5
- first_shift: bfloat16 [768], P('seq'), may hold values from -4 to 4
- joint_weight: bfloat16 [768, 2304], P('seq'), may hold values from -0.3125 to 0.3125
- output_weight: bfloat16 [768, 768], P('seq'), may hold values from -0.875 to 0.875
- second_gain: bfloat16 [768], P('seq'), may hold values from 0.5 to 1.5
- second_shift: bfloat16 [768], P('seq'), may hold values from -4 to 4
- up_weight: bfloat16 [768, 3072], P('seq'), may hold values from -0.21875 to 0.21875
- up_bias: bfloat16 [3072], P('seq'), may hold values from -6 to 6
- down_weight: bfloat16 [3072, 768], P('seq'), may hold values from -0.109375 to 0.109375
- down_bias: bfloat16 [768], P('seq'), may hold values from -6 to 6
- block_number: int32 [4, 4096], P('dp'), may hold values from 0 to 31, never falling along the last dimension, each value on 1 to 256 neighbouring positions
- cotangent: bfloat16 [4, 4096, 768], P('dp', 'seq'), may hold values from -6 to 6
Outputs:
- block_output: bfloat16 [4, 4096, 768], P('dp', 'seq')
- patches_gradient: bfloat16 [4, 4096, 6144], P('dp', 'seq')
- embedding_gradient: float32 [6144, 768], P('seq')
- first_gain_gradient: float32 [768], P('seq')
- first_shift_gradient: float32 [768], P('seq')
- joint_weight_gradient: float32 [768, 2304], P('seq')
- output_weight_gradient: float32 [768, 768], P('seq')
- second_gain_gradient: float32 [768], P('seq')
- second_shift_gradient: float32 [768], P('seq')
- up_weight_gradient: float32 [768, 3072], P('seq')
- up_bias_gradient: float32 [3072], P('seq')
- down_weight_gradient: float32 [3072, 768], P('seq')
- down_bias_gradient: float32 [768], P('seq')
The draws below stay inside these ranges and needn't reach their ends.
Inputs may be any that keep to these rules, and one draw needn't show every extreme that they name: `block_number`: in each sequence the block numbers never fall along the rows; each block has 1 to 256 rows, and some block has exactly 256.
All inputs are finite; a program needn't handle non-finite values.
Results may differ from the reference program's by a relative error of at most 0.038.
Values may be sent and summed in bfloat16 or wider, within the bound.
No kernel may reach another device: no remote copies, remote signals or barrier semaphores. Data moves between devices by JAX's collectives and lax.ppermute only.
A program may use at most 256 MiB of HBM per device.

```python
import math
import jax
import jax.numpy as jnp
import numpy as np
from jax import lax

D = 768
HEADS = 12
HEAD_DIM = 64
FF = 3072
BLOCK = 256
IN = 6144
LEN = 4096
NSEQ = 4
NBLK = 32


def shard_levels(rng, shape, cuts, low, largest):
    def one(axis_at, shards_of):
        heights = jax.random.uniform(jax.random.fold_in(jax.random.fold_in(rng, 6), axis_at), (shards_of,), jnp.float32, low / len(cuts), largest / len(cuts))
        return jnp.repeat(jnp.exp(heights), shape[axis_at] // shards_of).reshape((-1,) + (1,) * (len(shape) - axis_at - 1))

    factor_of = one(*cuts[0])
    for cut in cuts[1:]:
        factor_of = factor_of * one(*cut)
    return factor_of


def split_up(number_of, total, reach, skew):
    loads = [(1 << 20) // math.isqrt(rank ** skew) + 1 for rank in range(2, number_of + 1)]
    spare, holding = total - reach - (number_of - 1), [1] * (number_of - 1)
    while spare > 0:
        movable = [i for i in range(number_of - 1) if holding[i] < reach]
        whole, left = sum([loads[i] for i in movable]), spare
        for i in movable:
            addition = min(reach - holding[i], max(1, left * loads[i] // whole), spare)
            holding[i] = holding[i] + addition
            spare = spare - addition
    return np.array([reach] + holding)


def uneven_parts(own_key, number_of, total, bound, skew):
    if number_of == 2:
        one = jax.random.randint(own_key, (), max(1, total - bound), min(bound, total - 1) + 1)
        return jnp.stack([one, total - one])
    sizes = jnp.asarray(split_up(number_of, total, bound, skew), jnp.int32)
    twos = (number_of - 1) // 2
    giver, receiver = sizes[1:1 + 2 * twos:2], sizes[2:2 + 2 * twos:2]
    margin = jnp.minimum(giver - 1, bound - receiver)
    passed = jax.random.randint(jax.random.fold_in(own_key, 1), (twos,), 0, 1 << 20) % (margin + 1)
    sizes = sizes.at[1:1 + 2 * twos:2].set(giver - passed).at[2:2 + 2 * twos:2].set(receiver + passed)
    return sizes[jax.random.permutation(jax.random.fold_in(own_key, 2), number_of)]


def bell_draw(stream_key, extent, scale, limit, split=(), dtype=jnp.bfloat16):
    values = scale * jax.random.normal(stream_key, extent, jnp.float32)
    if split:
        values = values * shard_levels(stream_key, extent, split, -0.22, 0.18)
    return jnp.clip(values, -limit, limit).astype(dtype)


def setup_inputs(seed: int = 0) -> dict:
    streams_of = jax.random.split(jax.random.key(seed), 15)
    patches = bell_draw(streams_of[0], (NSEQ, LEN, IN), 1.0, 6.0, ((0, 4), (1, 8)))
    embedding = bell_draw(streams_of[1], (IN, D), IN ** -0.5, 0.078125, ((0, 8),))
    first_gain = jnp.clip(1.0 + 0.1 * jax.random.normal(streams_of[2], (D,), jnp.float32), 0.5, 1.5).astype(jnp.bfloat16)
    first_shift = bell_draw(streams_of[3], (D,), 0.3, 4.0, ((0, 8),))
    joint_weight = bell_draw(streams_of[4], (D, 3 * D), (D // 2) ** -0.5, 0.3125, ((0, 8),))
    output_weight = bell_draw(streams_of[5], (D, D), (D // 16) ** -0.5, 0.875, ((0, 8),))
    second_gain = jnp.clip(1.0 + 0.1 * jax.random.normal(streams_of[6], (D,), jnp.float32), 0.5, 1.5).astype(jnp.bfloat16)
    second_shift = bell_draw(streams_of[7], (D,), 0.3, 4.0, ((0, 8),))
    up_weight = bell_draw(streams_of[8], (D, FF), D ** -0.5, 0.21875, ((0, 8),))
    up_bias = bell_draw(streams_of[9], (FF,), 0.5, 6.0, ((0, 8),))
    down_weight = bell_draw(streams_of[10], (FF, D), FF ** -0.5, 0.109375, ((0, 8),))
    down_bias = bell_draw(streams_of[11], (D,), 0.5, 6.0, ((0, 8),))
    block_number = jax.vmap(lambda own: jnp.searchsorted(jnp.cumsum(uneven_parts(own, NBLK, LEN, BLOCK, 1)), jnp.arange(LEN), side="right"))(jax.random.split(streams_of[12], NSEQ)).reshape((NSEQ, LEN)).astype(jnp.int32)
    cotangent = bell_draw(streams_of[13], (NSEQ, LEN, D), 1.0, 6.0, ((0, 4), (1, 8)))
    return dict(patches=patches, embedding=embedding, first_gain=first_gain, first_shift=first_shift, joint_weight=joint_weight, output_weight=output_weight, second_gain=second_gain, second_shift=second_shift, up_weight=up_weight, up_bias=up_bias, down_weight=down_weight, down_bias=down_bias, block_number=block_number, cotangent=cotangent)


@jax.custom_vjp
def low(v):
    return lax.optimization_barrier(v.astype(jnp.bfloat16)).astype(jnp.float32)

@jax.custom_vjp
def low_back(v):
    return v

def low_keep(v):
    return (low(v), None)

def low_pass(kept, grad):
    return (grad,)

def back_keep(v):
    return (v, None)

def back_low(kept, grad):
    return (low(grad),)
low.defvjp(low_keep, low_pass)
low_back.defvjp(back_keep, back_low)
EPS = 1e-05
NEG = -1e+30
HIGH = lax.Precision.HIGHEST

def layer_norm(values, gain, shift):
    center = values - lax.optimization_barrier(jnp.mean(values, axis=-1, keepdims=True))
    spread = lax.optimization_barrier(jnp.mean(center * center, axis=-1, keepdims=True))
    return center * lax.rsqrt(spread + EPS) * gain + shift

def product(left, right):
    return jnp.dot(left, right, precision=HIGH, preferred_element_type=jnp.float32)

def attention(query, keys, values, row_ids):
    length = query.shape[0]
    width = math.gcd(length, 512)
    scale = HEAD_DIM ** (-0.5)
    query_blocks = query.reshape(length // width, width, HEADS, HEAD_DIM)
    id_blocks = row_ids.reshape(length // width, width)

    @jax.checkpoint
    def one_block(pieces):
        rows, block_ids = pieces
        scores = low_back(scale * jnp.einsum('qhd,khd->hqk', rows, keys, precision=HIGH))
        visible = row_ids[None, None, :] <= block_ids[None, :, None]
        probs = low(jax.nn.softmax(jnp.where(visible, scores, NEG), axis=-1))
        return jnp.einsum('hqk,khd->qhd', probs, values, precision=HIGH)
    result = lax.map(one_block, (query_blocks, id_blocks))
    return result.reshape(length, HEADS * HEAD_DIM)

def forward(inputs, params, row_ids):
    embedding, first_gain, first_shift, joint_weight, output_weight, second_gain, second_shift, up_weight, up_bias, down_weight, down_bias = params
    length = inputs.shape[0]
    model = HEADS * HEAD_DIM
    hidden = low_back(product(inputs, embedding))
    normed1 = low(layer_norm(hidden, first_gain, first_shift))
    joint = low_back(low(product(normed1, joint_weight)))
    query = joint[:, :model].reshape(length, HEADS, HEAD_DIM)
    keys = joint[:, model:2 * model].reshape(length, HEADS, HEAD_DIM)
    values = joint[:, 2 * model:].reshape(length, HEADS, HEAD_DIM)
    attended = low_back(low(attention(query, keys, values, row_ids)))
    mixed = low_back(product(attended, output_weight))
    resid = hidden + mixed
    normed2 = low(layer_norm(resid, second_gain, second_shift))
    upper = low_back(product(normed2, up_weight) + up_bias)
    gate = low(jax.nn.gelu(upper, approximate=True))
    lowered = low_back(product(gate, down_weight) + down_bias)
    return resid + lowered

def reference(patches, embedding, first_gain, first_shift, joint_weight, output_weight, second_gain, second_shift, up_weight, up_bias, down_weight, down_bias, block_number, cotangent):
    weights = tuple((w.astype(jnp.float32) for w in (embedding, first_gain, first_shift, joint_weight, output_weight, second_gain, second_shift, up_weight, up_bias, down_weight, down_bias)))

    def one_sequence(totals, pieces):
        rows, row_ids, tangent = pieces
        row_ids = row_ids.astype(jnp.int32)

        def apply(inputs, *params):
            return forward(inputs, params, row_ids)
        outcome, pull = jax.vjp(apply, rows.astype(jnp.float32), *weights)
        grads = pull(tangent.astype(jnp.float32))
        totals = tuple((t + g for t, g in zip(totals, grads[1:])))
        return (totals, (outcome.astype(jnp.bfloat16), grads[0].astype(jnp.bfloat16)))
    zeros = tuple((jnp.zeros_like(w) for w in weights))
    totals, (outputs, patch_grads) = lax.scan(one_sequence, zeros, (patches, block_number, cotangent))
    return (outputs, patch_grads, totals[0], totals[1], totals[2], totals[3], totals[4], totals[5], totals[6], totals[7], totals[8], totals[9], totals[10])
```

```python
import functools
import math

import jax
import jax.numpy as jnp
from jax import lax
from jax.experimental import pallas as pl
from jax.experimental.pallas import tpu as pltpu
from jax.sharding import PartitionSpec as P

AXES = ("dp", "seq")
EPS = 1e-05
HEAD_DIM = 64
GROUPS = 4
PER = 3
EDGE = 256
NEG = -1e30
SCALE = HEAD_DIM ** (-0.5)
LOG2E = math.log2(math.e)
SCALE2 = SCALE * LOG2E


def slot_of(place_ref, part, width):
    own_group, own_part = place_ref[0], place_ref[1]
    group, inner = part // width, part % width
    return (own_part - inner + width) % width, (own_group - group + GROUPS) % GROUPS


def forward_kernel(width, place_ref, query_ref, pair_ref, ends_ref, out_ref, log_ref, keys, top, total, accum):
    step = pl.program_id(0)
    rows = query_ref.shape[-1]
    parts = width * GROUPS

    @pl.when(step == 0)
    def _():
        def turn(at, carry):
            for head in range(PER):
                keys[at * PER + head] = pair_ref[at // GROUPS, at % GROUPS, 0, head].T
            return carry

        lax.fori_loop(0, parts, turn, 0)

    own = ((place_ref[0] - step + GROUPS) % GROUPS) * width + place_ref[1]

    def tile(part, kspan, qspan, masked, first):
        inner, group = slot_of(place_ref, part, width)
        slot = inner * GROUPS + group
        k0, kn = kspan
        q0, qn = qspan
        for head in range(PER):
            scores = jnp.dot(
                keys[slot * PER + head, k0 : k0 + kn, :],
                query_ref[0, head, :, q0 : q0 + qn],
                preferred_element_type=jnp.float32,
            )
            if masked:
                at = part * rows + k0 + lax.broadcasted_iota(jnp.int32, (kn, qn), 0)
                scores = jnp.where(at < ends_ref[own, :, q0 : q0 + qn], scores, NEG)
            new_top = jnp.max(scores, axis=0, keepdims=True) * SCALE2
            if not first:
                old_top = top[head, :, q0 : q0 + qn]
                new_top = jnp.maximum(old_top, new_top)
            weights = jnp.exp2(scores * SCALE2 - new_top)
            added = jnp.sum(weights, axis=0, keepdims=True)
            mixed = jnp.dot(
                pair_ref[inner, group, 1, head, :, k0 : k0 + kn],
                weights.astype(jnp.bfloat16),
                preferred_element_type=jnp.float32,
            )
            if first:
                total[head, :, q0 : q0 + qn] = added
                accum[head, :, q0 : q0 + qn] = mixed
            else:
                shrink = jnp.exp2(old_top - new_top)
                total[head, :, q0 : q0 + qn] = total[head, :, q0 : q0 + qn] * shrink + added
                accum[head, :, q0 : q0 + qn] = accum[head, :, q0 : q0 + qn] * shrink + mixed
            top[head, :, q0 : q0 + qn] = new_top

    tile(own, (0, rows), (0, rows), True, True)

    @pl.when(jnp.logical_and(own + 1 < parts, place_ref[2 + own] > (own + 1) * rows))
    def _():
        tile(own + 1, (0, EDGE), (rows - EDGE, EDGE), True, False)

    def whole(part, carry):
        tile(part, (0, rows), (0, rows), False, False)
        return carry

    lax.fori_loop(0, own, whole, 0)
    for head in range(PER):
        out_ref[0, head] = (accum[head] / total[head]).astype(jnp.bfloat16)
        log_ref[0, head] = top[head] + jnp.log2(total[head])


def attention_forward(place, query, pairs, ends):
    width, rows = pairs.shape[0], query.shape[-1]
    parts = width * GROUPS
    block = (1, PER, HEAD_DIM, rows)
    return pl.pallas_call(
        functools.partial(forward_kernel, width),
        grid_spec=pltpu.PrefetchScalarGridSpec(
            num_scalar_prefetch=1,
            grid=(GROUPS,),
            in_specs=[
                pl.BlockSpec(block, lambda i, p: (i, 0, 0, 0)),
                pl.BlockSpec(pairs.shape, lambda i, p: (0, 0, 0, 0, 0, 0)),
                pl.BlockSpec(ends.shape, lambda i, p: (0, 0, 0)),
            ],
            out_specs=[
                pl.BlockSpec(block, lambda i, p: (i, 0, 0, 0)),
                pl.BlockSpec((1, PER, 1, rows), lambda i, p: (i, 0, 0, 0)),
            ],
            scratch_shapes=[
                pltpu.VMEM((parts * PER, rows, HEAD_DIM), jnp.bfloat16),
                pltpu.VMEM((PER, 1, rows), jnp.float32),
                pltpu.VMEM((PER, 1, rows), jnp.float32),
                pltpu.VMEM((PER, HEAD_DIM, rows), jnp.float32),
            ],
        ),
        out_shape=[
            jax.ShapeDtypeStruct(query.shape, jnp.bfloat16),
            jax.ShapeDtypeStruct((GROUPS, PER, 1, rows), jnp.float32),
        ],
        name="attention_forward",
    )(place, query, pairs, ends)


def backward_kernel(
    width, place_ref, query_ref, pair_ref, ends_ref, log_ref, out_ref, grad_ref,
    dquery_ref, dpair_ref, keys, values, dkeys, dvalues, query_turned, grad_turned, delta, dquery,
):
    step = pl.program_id(0)
    rows = query_ref.shape[-1]
    parts = width * GROUPS

    @pl.when(step == 0)
    def _():
        def turn(at, carry):
            for head in range(PER):
                keys[at * PER + head] = pair_ref[at // GROUPS, at % GROUPS, 0, head].T
                values[at * PER + head] = pair_ref[at // GROUPS, at % GROUPS, 1, head].T
                dkeys[at * PER + head] = jnp.zeros((rows, HEAD_DIM), jnp.float32)
                dvalues[at * PER + head] = jnp.zeros((rows, HEAD_DIM), jnp.float32)
            return carry

        lax.fori_loop(0, parts, turn, 0)

    own = ((place_ref[0] - step + GROUPS) % GROUPS) * width + place_ref[1]
    for head in range(PER):
        query_turned[head] = query_ref[0, head].T
        grad_turned[head] = grad_ref[0, head].T
        delta[head] = jnp.sum(
            grad_ref[0, head].astype(jnp.float32) * out_ref[0, head].astype(jnp.float32),
            axis=0,
            keepdims=True,
        )
        dquery[head] = jnp.zeros((HEAD_DIM, rows), jnp.float32)

    def tile(part, kspan, qspan, masked):
        inner, group = slot_of(place_ref, part, width)
        slot = inner * GROUPS + group
        k0, kn = kspan
        q0, qn = qspan
        for head in range(PER):
            at_slot = slot * PER + head
            scores = jnp.dot(
                keys[at_slot, k0 : k0 + kn, :],
                query_ref[0, head, :, q0 : q0 + qn],
                preferred_element_type=jnp.float32,
            )
            if masked:
                at = part * rows + k0 + lax.broadcasted_iota(jnp.int32, (kn, qn), 0)
                scores = jnp.where(at < ends_ref[own, :, q0 : q0 + qn], scores, NEG)
            weights = jnp.exp2(scores * SCALE2 - log_ref[0, head, :, q0 : q0 + qn])
            dweights = jnp.dot(
                values[at_slot, k0 : k0 + kn, :],
                grad_ref[0, head, :, q0 : q0 + qn],
                preferred_element_type=jnp.float32,
            )
            dscores = (weights * (dweights - delta[head, :, q0 : q0 + qn])).astype(jnp.bfloat16)
            dvalues[at_slot, k0 : k0 + kn, :] += jnp.dot(
                weights.astype(jnp.bfloat16),
                grad_turned[head, q0 : q0 + qn, :],
                preferred_element_type=jnp.float32,
            )
            dkeys[at_slot, k0 : k0 + kn, :] += jnp.dot(
                dscores, query_turned[head, q0 : q0 + qn, :], preferred_element_type=jnp.float32
            )
            dquery[head, :, q0 : q0 + qn] += jnp.dot(
                pair_ref[inner, group, 0, head, :, k0 : k0 + kn],
                dscores,
                preferred_element_type=jnp.float32,
            )

    tile(own, (0, rows), (0, rows), True)

    @pl.when(jnp.logical_and(own + 1 < parts, place_ref[2 + own] > (own + 1) * rows))
    def _():
        tile(own + 1, (0, EDGE), (rows - EDGE, EDGE), True)

    def whole(part, carry):
        tile(part, (0, rows), (0, rows), False)
        return carry

    lax.fori_loop(0, own, whole, 0)
    for head in range(PER):
        dquery_ref[0, head] = (dquery[head] * SCALE).astype(jnp.bfloat16)

    @pl.when(step == GROUPS - 1)
    def _():
        def give(at, carry):
            for head in range(PER):
                dpair_ref[at // GROUPS, at % GROUPS, 0, head] = (
                    (dkeys[at * PER + head] * SCALE).T.astype(jnp.bfloat16)
                )
                dpair_ref[at // GROUPS, at % GROUPS, 1, head] = (
                    dvalues[at * PER + head].T.astype(jnp.bfloat16)
                )
            return carry

        lax.fori_loop(0, parts, give, 0)


def attention_backward(place, query, pairs, ends, logs, out, grad):
    width, rows = pairs.shape[0], query.shape[-1]
    parts = width * GROUPS
    block = (1, PER, HEAD_DIM, rows)
    own_block = pl.BlockSpec(block, lambda i, p: (i, 0, 0, 0))
    whole_pairs = pl.BlockSpec(pairs.shape, lambda i, p: (0, 0, 0, 0, 0, 0))
    return pl.pallas_call(
        functools.partial(backward_kernel, width),
        grid_spec=pltpu.PrefetchScalarGridSpec(
            num_scalar_prefetch=1,
            grid=(GROUPS,),
            in_specs=[
                own_block,
                whole_pairs,
                pl.BlockSpec(ends.shape, lambda i, p: (0, 0, 0)),
                pl.BlockSpec((1, PER, 1, rows), lambda i, p: (i, 0, 0, 0)),
                own_block,
                own_block,
            ],
            out_specs=[own_block, whole_pairs],
            scratch_shapes=[
                pltpu.VMEM((parts * PER, rows, HEAD_DIM), jnp.bfloat16),
                pltpu.VMEM((parts * PER, rows, HEAD_DIM), jnp.bfloat16),
                pltpu.VMEM((parts * PER, rows, HEAD_DIM), jnp.float32),
                pltpu.VMEM((parts * PER, rows, HEAD_DIM), jnp.float32),
                pltpu.VMEM((PER, rows, HEAD_DIM), jnp.bfloat16),
                pltpu.VMEM((PER, rows, HEAD_DIM), jnp.bfloat16),
                pltpu.VMEM((PER, 1, rows), jnp.float32),
                pltpu.VMEM((PER, HEAD_DIM, rows), jnp.float32),
            ],
        ),
        out_shape=[
            jax.ShapeDtypeStruct(query.shape, jnp.bfloat16),
            jax.ShapeDtypeStruct(pairs.shape, jnp.bfloat16),
        ],
        name="attention_backward",
    )(place, query, pairs, ends, logs, out, grad)


def gelu_parts(upper):
    inner = math.sqrt(2 / math.pi) * (upper + 0.044715 * upper * upper * upper)
    bent = jnp.tanh(inner)
    value = 0.5 * upper * (1 + bent)
    slope = 0.5 * (1 + bent) + 0.5 * upper * (1 - bent * bent) * math.sqrt(2 / math.pi) * (
        1 + 3 * 0.044715 * upper * upper
    )
    return value, slope


def mlp_kernel(low_ref, low_turned_ref, tangent_ref, weight_ref, bias_ref, lowered_ref, back_ref, dweight_ref, dbias_ref):
    step = pl.program_id(0)
    shards, both, model = weight_ref.shape[1:]
    half = both // 2
    up = weight_ref[0, :, :half, :].reshape(model, model)
    down = weight_ref[0, :, half:, :].reshape(model, model)
    tangent = tangent_ref[...]
    upper = jnp.dot(low_ref[...], up, preferred_element_type=jnp.float32) + bias_ref[0]
    value, slope = gelu_parts(upper)
    gate = value.astype(jnp.bfloat16)
    lowered = jnp.dot(gate, down, preferred_element_type=jnp.float32)
    gate_grad = lax.dot_general(
        tangent, down, (((1,), (1,)), ((), ())), preferred_element_type=jnp.float32
    )
    upper_grad = (gate_grad * slope).astype(jnp.bfloat16)
    back = lax.dot_general(
        upper_grad, up, (((1,), (1,)), ((), ())), preferred_element_type=jnp.float32
    )
    dup = jnp.dot(low_turned_ref[...], upper_grad, preferred_element_type=jnp.float32)
    ddown = jnp.dot(gate.T, tangent, preferred_element_type=jnp.float32)
    dweight_ref[0, :, 0, :half, :] = dup.astype(jnp.bfloat16).reshape(shards, half, model)
    dweight_ref[0, :, 0, half:, :] = ddown.astype(jnp.bfloat16).reshape(shards, half, model)
    dbias_ref[0] = jnp.sum(upper_grad.astype(jnp.float32), axis=0, keepdims=True)

    @pl.when(step == 0)
    def _():
        lowered_ref[...] = lowered
        back_ref[...] = back

    @pl.when(step > 0)
    def _():
        lowered_ref[...] += lowered
        back_ref[...] += back


def mlp(low, low_turned, tangent, weights, bias):
    rows, model = low.shape
    groups, shards, both, _ = weights.shape
    resident = pl.BlockSpec((rows, model), lambda i: (0, 0))
    stream = pl.BlockSpec((1, shards, both, model), lambda i: (i, 0, 0, 0))
    small = pl.BlockSpec((1, 1, model), lambda i: (i, 0, 0))
    return pl.pallas_call(
        mlp_kernel,
        grid=(groups,),
        in_specs=[resident, pl.BlockSpec((model, rows), lambda i: (0, 0)), resident, stream, small],
        out_specs=[
            resident,
            resident,
            pl.BlockSpec((1, shards, 1, both, model), lambda i: (i // 2, 0, i % 2, 0, 0)),
            small,
        ],
        out_shape=[
            jax.ShapeDtypeStruct((rows, model), jnp.float32),
            jax.ShapeDtypeStruct((rows, model), jnp.float32),
            jax.ShapeDtypeStruct((2, shards, groups // 2, both, model), jnp.bfloat16),
            jax.ShapeDtypeStruct((groups, 1, model), jnp.float32),
        ],
        name="mlp",
    )(low, low_turned, tangent, weights, bias)


def norm_forward(values, gain, shift):
    center = values - jnp.mean(values, axis=-1, keepdims=True)
    inverse = lax.rsqrt(jnp.mean(center * center, axis=-1, keepdims=True) + EPS)
    scaled = center * inverse
    return (scaled * gain + shift).astype(jnp.bfloat16), scaled, inverse


def norm_backward(grad, scaled, inverse, gain):
    inner = grad * gain
    back = inverse * (
        inner
        - jnp.mean(inner, axis=-1, keepdims=True)
        - scaled * jnp.mean(inner * scaled, axis=-1, keepdims=True)
    )
    return back, jnp.sum(grad * scaled, axis=0), jnp.sum(grad, axis=0)


def per_device(groups_dp, shards, *arguments):
    (
        patches, embedding, first_gain, first_shift, joint_weight, output_weight,
        second_gain, second_shift, up_weight, up_bias, down_weight, down_bias,
        block_number, cotangent,
    ) = arguments
    f32, bf16 = jnp.float32, jnp.bfloat16
    _, rows, width_in = patches.shape
    model = output_weight.shape[1]
    length = block_number.shape[1]
    unit = model // shards
    hidden_units = up_weight.shape[1]
    piece = hidden_units // (GROUPS * shards)
    embed_rows = embedding.shape[0]
    width = shards // GROUPS
    fast = groups_dp == 4 and shards % GROUPS == 0
    dp, seq = lax.axis_index("dp"), lax.axis_index("seq")
    core, own_group, own_part = dp % 2, seq // width, seq % width
    feature = model // GROUPS

    everyone = [(d, s) for d in range(groups_dp) for s in range(shards)]

    def moved(value, rule):
        pairs = []
        for d, s in everyone:
            there = rule(d, s)
            pairs.append((d * shards + s, there[0] * shards + there[1]))
        return lax.ppermute(value, AXES, pairs)

    def along_groups(value, by):
        return moved(value, lambda d, s: (d, ((s // width + by) % GROUPS) * width + s % width))

    def along_parts(value, by):
        return moved(value, lambda d, s: (d, (s // width) * width + (s % width + by) % width))

    def to_core(value):
        return moved(value, lambda d, s: (d ^ 1, s))

    def to_chip(value):
        return moved(value, lambda d, s: (d ^ 2, s))

    def gathered(quarters):
        if fast:
            mine = lax.dynamic_index_in_dim(quarters, dp, 0, keepdims=False)
            whole = lax.all_gather(mine, AXES, axis=0, tiled=False)
            return whole.reshape(GROUPS, shards, *mine.shape)
        whole = lax.all_gather(quarters, "seq", axis=0, tiled=False)
        return jnp.swapaxes(whole, 0, 1)

    vectors = jnp.concatenate([first_gain, first_shift, second_gain, second_shift, down_bias, up_bias])
    count = vectors.shape[0]
    extra = 16
    vector_rows = jnp.pad(vectors, (0, extra * feature - count)).reshape(extra, feature)
    embed_quarters = jnp.swapaxes(embedding.reshape(embed_rows, GROUPS, feature), 0, 1)
    embed_packed = jnp.concatenate(
        [embed_quarters, jnp.broadcast_to(vector_rows, (GROUPS, extra, feature))], axis=1
    )
    embed_all = gathered(embed_packed)
    joint_quarters = jnp.transpose(
        joint_weight.reshape(unit, 3, GROUPS, feature), (2, 0, 1, 3)
    ).reshape(GROUPS, unit, 3 * feature)
    joint_full = gathered(joint_quarters).reshape(GROUPS, model, 3 * feature)
    output_all = gathered(output_weight.reshape(GROUPS, unit // GROUPS, model))
    output_full = jnp.swapaxes(output_all, 0, 1).reshape(model, model)
    up_quarters = jnp.transpose(
        up_weight.reshape(unit, shards, GROUPS, piece), (2, 0, 1, 3)
    ).reshape(GROUPS, unit, model)
    mlp_full = gathered(
        jnp.concatenate([up_quarters, down_weight.reshape(GROUPS, piece, model)], axis=1)
    )

    embed_full = jnp.transpose(embed_all[:, :, :embed_rows], (1, 2, 0, 3)).reshape(width_in, model)
    vector_all = embed_all[0, :, embed_rows:].reshape(shards, extra * feature)[:, :count].astype(f32)

    def vector_of(at, size):
        return vector_all[:, at * unit : at * unit + size]

    gain_one, shift_one, gain_two, shift_two, bias_down = (
        vector_of(at, unit).reshape(1, model) for at in range(5)
    )
    bias_up = jnp.transpose(
        vector_of(5, GROUPS * piece).reshape(shards, GROUPS, piece), (1, 0, 2)
    ).reshape(GROUPS, 1, model)

    ids = block_number[0]
    ends = jnp.sum((ids[None, :] <= ids[:, None]).astype(jnp.int32), axis=1)
    ends = ends.reshape(shards, 1, rows)
    place = jnp.concatenate([jnp.stack([own_group, own_part]).astype(jnp.int32), ends[:, 0, -1]])

    flat_in = patches[0]
    tangent = cotangent[0]
    hidden = jnp.dot(flat_in, embed_full, preferred_element_type=f32)
    normed1, scaled1, inverse1 = norm_forward(hidden, gain_one, shift_one)
    joint = jnp.einsum("gkn,rk->gnr", joint_full, normed1, preferred_element_type=f32).astype(bf16)

    def scattered(value):
        got = [lax.dynamic_index_in_dim(value, own_group, 0, keepdims=False)]
        for by in range(1, GROUPS):
            part = lax.dynamic_index_in_dim(value, (own_group + by) % GROUPS, 0, keepdims=False)
            got.append(along_groups(part, by))
        return got

    def returned(parts):
        whole = jnp.zeros((GROUPS, *parts[0].shape), parts[0].dtype)
        for by in range(GROUPS):
            part = parts[by] if by == 0 else along_groups(parts[by], GROUPS - by)
            whole = lax.dynamic_update_index_in_dim(whole, part, (own_group + by) % GROUPS, 0)
        return whole

    arrived = scattered(joint)
    halves = [part[feature:] for part in arrived]
    own_pairs = jnp.stack(halves)
    every_pair = [own_pairs]
    for by in range(1, width):
        every_pair.append(jnp.stack([along_parts(part, by) for part in halves]))
    pairs = jnp.stack(every_pair).reshape(width, GROUPS, 2, PER, HEAD_DIM, rows)
    query = jnp.stack([part[:feature] for part in arrived]).reshape(GROUPS, PER, HEAD_DIM, rows)
    out, logs = attention_forward(place, query, pairs, ends)
    flat_out = out.reshape(GROUPS, feature, rows)
    attended = returned([flat_out[by] for by in range(GROUPS)]).reshape(model, rows)

    resid = hidden + lax.dot_general(
        attended, output_full, (((0,), (0,)), ((), ())), preferred_element_type=f32
    )
    normed2, scaled2, inverse2 = norm_forward(resid, gain_two, shift_two)
    lowered, normed2_grad, mlp_grad, bias_up_grad = mlp(normed2, normed2.T, tangent, mlp_full, bias_up)
    block_output = (resid + lowered + bias_down).astype(bf16)[None]

    tangent_wide = tangent.astype(f32)
    resid_back, gain_two_grad, shift_two_grad = norm_backward(normed2_grad, scaled2, inverse2, gain_two)
    resid_grad = tangent_wide + resid_back
    mixed_grad = resid_grad.astype(bf16)
    attended_grad = lax.dot_general(
        output_full, mixed_grad, (((1,), (1,)), ((), ())), preferred_element_type=f32
    ).astype(bf16)
    grad_parts = scattered(attended_grad.reshape(GROUPS, feature, rows))
    grad_in = jnp.stack(grad_parts).reshape(GROUPS, PER, HEAD_DIM, rows)
    dquery, dpairs = attention_backward(place, query, pairs, ends, logs, out, grad_in)
    dpair_own = dpairs[0].reshape(GROUPS, 2 * feature, rows)
    if width > 1:
        total = dpair_own.astype(f32)
        for by in range(1, width):
            total = total + along_parts(dpairs[by].reshape(GROUPS, 2 * feature, rows), width - by).astype(f32)
        dpair_own = total.astype(bf16)
    joint_back = jnp.concatenate([dquery.reshape(GROUPS, feature, rows), dpair_own], axis=1)
    joint_grad = returned([joint_back[by] for by in range(GROUPS)])

    def reduced(halves):
        if not fast:
            both = jnp.stack(halves, axis=1)
            mine = lax.psum(lax.psum_scatter(both, "seq", scatter_dimension=0, tiled=False), "dp")
            return mine[0].astype(f32), mine[1].astype(f32)
        pick = core == 0
        kept = jnp.where(pick, halves[0], halves[1])
        given = jnp.where(pick, halves[1], halves[0])
        both = (kept.astype(f32) + to_core(given).astype(f32)).astype(bf16)
        mine = lax.psum_scatter(both, "seq", scatter_dimension=0, tiled=False)
        mine = (mine.astype(f32) + to_chip(mine).astype(f32)).astype(bf16)
        other = to_core(mine)
        return (
            jnp.where(pick, mine, other).astype(f32),
            jnp.where(pick, other, mine).astype(f32),
        )

    mlp_halves = reduced(tuple(mlp_grad[at].reshape(shards, -1, model) for at in (0, 1)))
    mlp_shard = jnp.stack(mlp_halves).reshape(GROUPS, -1, model)
    up_grad = jnp.transpose(
        mlp_shard[:, :unit].reshape(GROUPS, unit, shards, piece), (1, 2, 0, 3)
    ).reshape(unit, hidden_units)
    down_grad = mlp_shard[:, unit:].reshape(GROUPS * piece, model)

    half = model // 2
    output_grad = jnp.dot(attended, mixed_grad, preferred_element_type=f32).astype(bf16)
    output_halves = reduced(
        tuple(output_grad[:, at : at + half].reshape(shards, unit, half) for at in (0, half))
    )
    output_shard = jnp.concatenate(output_halves, axis=-1)

    joint_weight_grad = jnp.einsum("rk,gnr->gkn", normed1, joint_grad, preferred_element_type=f32)
    joint_weight_grad = joint_weight_grad.astype(bf16).reshape(2, 2, shards, unit, 3 * feature)
    joint_halves = reduced(
        tuple(
            jnp.swapaxes(joint_weight_grad[at], 0, 1).reshape(shards, 2 * unit, 3 * feature) for at in (0, 1)
        )
    )
    joint_shard = jnp.transpose(
        jnp.stack(joint_halves).reshape(GROUPS, unit, 3, feature), (1, 2, 0, 3)
    ).reshape(unit, 3 * model)

    normed1_grad = jnp.einsum("gnr,gkn->rk", joint_grad, joint_full, preferred_element_type=f32)
    hidden_back, gain_one_grad, shift_one_grad = norm_backward(normed1_grad, scaled1, inverse1, gain_one)
    hidden_grad = (resid_grad + hidden_back).astype(bf16)
    embed_halves = reduced(
        tuple(
            lax.dot_general(
                flat_in, hidden_grad[:, at : at + half], (((0,), (0,)), ((), ())), preferred_element_type=f32
            )
            .astype(bf16)
            .reshape(shards, embed_rows, half)
            for at in (0, half)
        )
    )
    embed_shard = jnp.concatenate(embed_halves, axis=-1)
    patches_grad = lax.dot_general(
        hidden_grad, embed_full, (((1,), (1,)), ((), ())), preferred_element_type=f32
    ).astype(bf16)[None]

    tangent_sum = jnp.sum(tangent_wide, axis=0)
    bias_up_natural = jnp.transpose(bias_up_grad.reshape(GROUPS, shards, piece), (1, 0, 2))
    packed = jnp.concatenate(
        [
            piece_of.reshape(shards, -1)
            for piece_of in (gain_one_grad, shift_one_grad, gain_two_grad, shift_two_grad, tangent_sum, bias_up_natural)
        ],
        axis=1,
    )
    if fast and shards == 8:
        packed = packed + to_core(packed)
        packed = packed + to_chip(packed)
        for bit in (1, 2, 4):
            packed = packed + moved(packed, lambda d, s, bit=bit: (d, s ^ bit))
    else:
        packed = lax.psum(packed, AXES)
    own_vectors = lax.dynamic_index_in_dim(packed, seq, 0, keepdims=False)
    own = [own_vectors[at * unit : (at + 1) * unit] for at in range(5)]
    return (
        block_output,
        patches_grad,
        embed_shard,
        own[0],
        own[1],
        joint_shard,
        output_shard,
        own[2],
        own[3],
        up_grad,
        own_vectors[5 * unit :],
        down_grad,
        own[4],
    )


def solution(mesh):
    rows, columns, vector = P("dp", "seq", None), P("seq", None), P("seq")
    placed = (
        rows, columns, vector, vector, columns, columns, vector, vector,
        columns, vector, columns, vector, P("dp", None), rows,
    )
    given = (
        rows, rows, columns, vector, vector, columns, columns,
        vector, vector, columns, vector, columns, vector,
    )
    return jax.shard_map(
        functools.partial(per_device, mesh.shape["dp"], mesh.shape["seq"]),
        mesh=mesh,
        in_specs=placed,
        out_specs=given,
        check_vma=False,
    )
```

```python
import functools
import math

import jax
import jax.numpy as jnp
from jax import lax
from jax.experimental import pallas as pl
from jax.experimental.pallas import tpu as pltpu
from jax.sharding import PartitionSpec as P

AXES = ("dp", "seq")
EPS = 1e-05
HEAD_DIM = 64
GROUPS = 4
PER = 3
EDGE = 256
NEG = -1e30
SCALE = HEAD_DIM ** (-0.5)
LOG2E = math.log2(math.e)
SCALE2 = SCALE * LOG2E


def slot_of(place_ref, part, width):
    own_group, own_part = place_ref[0], place_ref[1]
    group, inner = part // width, part % width
    return (own_part - inner + width) % width, (own_group - group + GROUPS) % GROUPS


def forward_kernel(width, place_ref, query_ref, pair_ref, ends_ref, out_ref, log_ref, keys, top, total, accum):
    step = pl.program_id(0)
    rows = query_ref.shape[-1]
    parts = width * GROUPS

    @pl.when(step == 0)
    def _():
        def turn(at, carry):
            for head in range(PER):
                keys[at * PER + head] = pair_ref[at // GROUPS, at % GROUPS, 0, head].T
            return carry

        lax.fori_loop(0, parts, turn, 0)

    own = ((place_ref[0] - step + GROUPS) % GROUPS) * width + place_ref[1]

    def tile(part, kspan, qspan, masked, first):
        inner, group = slot_of(place_ref, part, width)
        slot = inner * GROUPS + group
        k0, kn = kspan
        q0, qn = qspan
        for head in range(PER):
            scores = jnp.dot(
                keys[slot * PER + head, k0 : k0 + kn, :],
                query_ref[0, head, :, q0 : q0 + qn],
                preferred_element_type=jnp.float32,
            )
            if masked:
                at = part * rows + k0 + lax.broadcasted_iota(jnp.int32, (kn, qn), 0)
                scores = jnp.where(at < ends_ref[own, :, q0 : q0 + qn], scores, NEG)
            new_top = jnp.max(scores, axis=0, keepdims=True) * SCALE2
            if not first:
                old_top = top[head, :, q0 : q0 + qn]
                new_top = jnp.maximum(old_top, new_top)
            weights = jnp.exp2(scores * SCALE2 - new_top)
            added = jnp.sum(weights, axis=0, keepdims=True)
            mixed = jnp.dot(
                pair_ref[inner, group, 1, head, :, k0 : k0 + kn],
                weights.astype(jnp.bfloat16),
                preferred_element_type=jnp.float32,
            )
            if first:
                total[head, :, q0 : q0 + qn] = added
                accum[head, :, q0 : q0 + qn] = mixed
            else:
                shrink = jnp.exp2(old_top - new_top)
                total[head, :, q0 : q0 + qn] = total[head, :, q0 : q0 + qn] * shrink + added
                accum[head, :, q0 : q0 + qn] = accum[head, :, q0 : q0 + qn] * shrink + mixed
            top[head, :, q0 : q0 + qn] = new_top

    tile(own, (0, rows), (0, rows), True, True)

    @pl.when(jnp.logical_and(own + 1 < parts, place_ref[2 + own] > (own + 1) * rows))
    def _():
        tile(own + 1, (0, EDGE), (rows - EDGE, EDGE), True, False)

    def whole(part, carry):
        tile(part, (0, rows), (0, rows), False, False)
        return carry

    lax.fori_loop(0, own, whole, 0)
    for head in range(PER):
        out_ref[0, head] = (accum[head] / total[head]).astype(jnp.bfloat16)
        log_ref[0, head] = top[head] + jnp.log2(total[head])


def attention_forward(place, query, pairs, ends):
    width, rows = pairs.shape[0], query.shape[-1]
    parts = width * GROUPS
    block = (1, PER, HEAD_DIM, rows)
    return pl.pallas_call(
        functools.partial(forward_kernel, width),
        grid_spec=pltpu.PrefetchScalarGridSpec(
            num_scalar_prefetch=1,
            grid=(GROUPS,),
            in_specs=[
                pl.BlockSpec(block, lambda i, p: (i, 0, 0, 0)),
                pl.BlockSpec(pairs.shape, lambda i, p: (0, 0, 0, 0, 0, 0)),
                pl.BlockSpec(ends.shape, lambda i, p: (0, 0, 0)),
            ],
            out_specs=[
                pl.BlockSpec(block, lambda i, p: (i, 0, 0, 0)),
                pl.BlockSpec((1, PER, 1, rows), lambda i, p: (i, 0, 0, 0)),
            ],
            scratch_shapes=[
                pltpu.VMEM((parts * PER, rows, HEAD_DIM), jnp.bfloat16),
                pltpu.VMEM((PER, 1, rows), jnp.float32),
                pltpu.VMEM((PER, 1, rows), jnp.float32),
                pltpu.VMEM((PER, HEAD_DIM, rows), jnp.float32),
            ],
        ),
        out_shape=[
            jax.ShapeDtypeStruct(query.shape, jnp.bfloat16),
            jax.ShapeDtypeStruct((GROUPS, PER, 1, rows), jnp.float32),
        ],
        name="attention_forward",
    )(place, query, pairs, ends)


def backward_kernel(
    width, place_ref, query_ref, pair_ref, ends_ref, log_ref, out_ref, grad_ref,
    dquery_ref, dpair_ref, keys, values, dkeys, dvalues, query_turned, grad_turned, delta, dquery,
):
    step = pl.program_id(0)
    rows = query_ref.shape[-1]
    parts = width * GROUPS

    @pl.when(step == 0)
    def _():
        def turn(at, carry):
            for head in range(PER):
                keys[at * PER + head] = pair_ref[at // GROUPS, at % GROUPS, 0, head].T
                values[at * PER + head] = pair_ref[at // GROUPS, at % GROUPS, 1, head].T
                dkeys[at * PER + head] = jnp.zeros((rows, HEAD_DIM), jnp.float32)
                dvalues[at * PER + head] = jnp.zeros((rows, HEAD_DIM), jnp.float32)
            return carry

        lax.fori_loop(0, parts, turn, 0)

    own = ((place_ref[0] - step + GROUPS) % GROUPS) * width + place_ref[1]
    for head in range(PER):
        query_turned[head] = query_ref[0, head].T
        grad_turned[head] = grad_ref[0, head].T
        delta[head] = jnp.sum(
            grad_ref[0, head].astype(jnp.float32) * out_ref[0, head].astype(jnp.float32),
            axis=0,
            keepdims=True,
        )
        dquery[head] = jnp.zeros((HEAD_DIM, rows), jnp.float32)

    def tile(part, kspan, qspan, masked):
        inner, group = slot_of(place_ref, part, width)
        slot = inner * GROUPS + group
        k0, kn = kspan
        q0, qn = qspan
        for head in range(PER):
            at_slot = slot * PER + head
            scores = jnp.dot(
                keys[at_slot, k0 : k0 + kn, :],
                query_ref[0, head, :, q0 : q0 + qn],
                preferred_element_type=jnp.float32,
            )
            if masked:
                at = part * rows + k0 + lax.broadcasted_iota(jnp.int32, (kn, qn), 0)
                scores = jnp.where(at < ends_ref[own, :, q0 : q0 + qn], scores, NEG)
            weights = jnp.exp2(scores * SCALE2 - log_ref[0, head, :, q0 : q0 + qn])
            dweights = jnp.dot(
                values[at_slot, k0 : k0 + kn, :],
                grad_ref[0, head, :, q0 : q0 + qn],
                preferred_element_type=jnp.float32,
            )
            dscores = (weights * (dweights - delta[head, :, q0 : q0 + qn])).astype(jnp.bfloat16)
            dvalues[at_slot, k0 : k0 + kn, :] += jnp.dot(
                weights.astype(jnp.bfloat16),
                grad_turned[head, q0 : q0 + qn, :],
                preferred_element_type=jnp.float32,
            )
            dkeys[at_slot, k0 : k0 + kn, :] += jnp.dot(
                dscores, query_turned[head, q0 : q0 + qn, :], preferred_element_type=jnp.float32
            )
            dquery[head, :, q0 : q0 + qn] += jnp.dot(
                pair_ref[inner, group, 0, head, :, k0 : k0 + kn],
                dscores,
                preferred_element_type=jnp.float32,
            )

    tile(own, (0, rows), (0, rows), True)

    @pl.when(jnp.logical_and(own + 1 < parts, place_ref[2 + own] > (own + 1) * rows))
    def _():
        tile(own + 1, (0, EDGE), (rows - EDGE, EDGE), True)

    def whole(part, carry):
        tile(part, (0, rows), (0, rows), False)
        return carry

    lax.fori_loop(0, own, whole, 0)
    for head in range(PER):
        dquery_ref[0, head] = (dquery[head] * SCALE).astype(jnp.bfloat16)

    @pl.when(step == GROUPS - 1)
    def _():
        def give(at, carry):
            for head in range(PER):
                dpair_ref[at // GROUPS, at % GROUPS, 0, head] = (
                    (dkeys[at * PER + head] * SCALE).T.astype(jnp.bfloat16)
                )
                dpair_ref[at // GROUPS, at % GROUPS, 1, head] = (
                    dvalues[at * PER + head].T.astype(jnp.bfloat16)
                )
            return carry

        lax.fori_loop(0, parts, give, 0)


def attention_backward(place, query, pairs, ends, logs, out, grad):
    width, rows = pairs.shape[0], query.shape[-1]
    parts = width * GROUPS
    block = (1, PER, HEAD_DIM, rows)
    own_block = pl.BlockSpec(block, lambda i, p: (i, 0, 0, 0))
    whole_pairs = pl.BlockSpec(pairs.shape, lambda i, p: (0, 0, 0, 0, 0, 0))
    return pl.pallas_call(
        functools.partial(backward_kernel, width),
        grid_spec=pltpu.PrefetchScalarGridSpec(
            num_scalar_prefetch=1,
            grid=(GROUPS,),
            in_specs=[
                own_block,
                whole_pairs,
                pl.BlockSpec(ends.shape, lambda i, p: (0, 0, 0)),
                pl.BlockSpec((1, PER, 1, rows), lambda i, p: (i, 0, 0, 0)),
                own_block,
                own_block,
            ],
            out_specs=[own_block, whole_pairs],
            scratch_shapes=[
                pltpu.VMEM((parts * PER, rows, HEAD_DIM), jnp.bfloat16),
                pltpu.VMEM((parts * PER, rows, HEAD_DIM), jnp.bfloat16),
                pltpu.VMEM((parts * PER, rows, HEAD_DIM), jnp.float32),
                pltpu.VMEM((parts * PER, rows, HEAD_DIM), jnp.float32),
                pltpu.VMEM((PER, rows, HEAD_DIM), jnp.bfloat16),
                pltpu.VMEM((PER, rows, HEAD_DIM), jnp.bfloat16),
                pltpu.VMEM((PER, 1, rows), jnp.float32),
                pltpu.VMEM((PER, HEAD_DIM, rows), jnp.float32),
            ],
        ),
        out_shape=[
            jax.ShapeDtypeStruct(query.shape, jnp.bfloat16),
            jax.ShapeDtypeStruct(pairs.shape, jnp.bfloat16),
        ],
        name="attention_backward",
    )(place, query, pairs, ends, logs, out, grad)


def gelu_parts(upper):
    inner = math.sqrt(2 / math.pi) * (upper + 0.044715 * upper * upper * upper)
    bent = jnp.tanh(inner)
    value = 0.5 * upper * (1 + bent)
    slope = 0.5 * (1 + bent) + 0.5 * upper * (1 - bent * bent) * math.sqrt(2 / math.pi) * (
        1 + 3 * 0.044715 * upper * upper
    )
    return value, slope


def embed_kernel(sizes, patches_ref, pieces_ref, gain_ref, shift_ref, hidden_ref, normed_ref, joint_ref, full_ref):
    step = pl.program_id(0)
    half_in, unit = sizes
    wide = pieces_ref.shape[-1]
    third = wide // 2
    parts = []
    for side in range(2):
        part = None
        for at in range(2):
            more = jnp.dot(
                patches_ref[:, at * half_in : (at + 1) * half_in],
                pieces_ref[at * 2 + side, 0, :half_in, :],
                preferred_element_type=jnp.float32,
            )
            part = more if part is None else part + more
        parts.append(part)
    for group in range(GROUPS):
        base = pl.multiple_of(step * unit, unit)
        middle = half_in + unit
        full_ref[group, pl.ds(base, unit), :wide] = pieces_ref[group, 0, half_in:middle, :]
        last = pieces_ref[group, 0, middle : middle + unit // 2, :]
        full_ref[group, pl.ds(base, unit // 2), wide:] = last[:, :third]
        full_ref[group, pl.ds(base + unit // 2, unit // 2), wide:] = last[:, third:]

    @pl.when(step == 0)
    def _():
        for side in range(2):
            hidden_ref[:, side * wide : (side + 1) * wide] = parts[side]

    @pl.when(step > 0)
    def _():
        for side in range(2):
            hidden_ref[:, side * wide : (side + 1) * wide] += parts[side]

    @pl.when(step == pl.num_programs(0) - 1)
    def _():
        normed = norm_forward(hidden_ref[...], gain_ref[...], shift_ref[...])[0]
        normed_ref[...] = normed
        for group in range(GROUPS):
            joint_ref[group] = (
                jnp.dot(normed, full_ref[group], preferred_element_type=jnp.float32).astype(jnp.bfloat16).T
            )


def embed(patches, pieces, gain, shift, unit):
    rows, width_in = patches.shape
    shards, model = pieces.shape[1], gain.shape[1]
    half_in = width_in // shards // 2
    wide = model // 2 * 3 // 2
    return pl.pallas_call(
        functools.partial(embed_kernel, (half_in, unit)),
        grid=(shards,),
        in_specs=[
            pl.BlockSpec((rows, 2 * half_in), lambda i: (0, i)),
            pl.BlockSpec((GROUPS, 1, *pieces.shape[2:]), lambda i: (0, i, 0, 0)),
            pl.BlockSpec((1, model), lambda i: (0, 0)),
            pl.BlockSpec((1, model), lambda i: (0, 0)),
        ],
        out_specs=[
            pl.BlockSpec((rows, model), lambda i: (0, 0)),
            pl.BlockSpec((rows, model), lambda i: (0, 0)),
            pl.BlockSpec((GROUPS, wide, rows), lambda i: (0, 0, 0)),
            pl.BlockSpec((GROUPS, model, wide), lambda i: (0, 0, 0)),
        ],
        out_shape=[
            jax.ShapeDtypeStruct((rows, model), jnp.float32),
            jax.ShapeDtypeStruct((rows, model), jnp.bfloat16),
            jax.ShapeDtypeStruct((GROUPS, wide, rows), jnp.bfloat16),
            jax.ShapeDtypeStruct((GROUPS, model, wide), jnp.bfloat16),
        ],
        name="embed",
    )(patches, pieces, gain, shift)


def patch_kernel(half_in, grad_ref, pieces_ref, out_ref):
    wide = pieces_ref.shape[-1]
    for at in range(2):
        part = None
        for side in range(2):
            more = lax.dot_general(
                grad_ref[:, side * wide : (side + 1) * wide],
                pieces_ref[at * 2 + side, 0, :half_in, :],
                (((1,), (1,)), ((), ())),
                preferred_element_type=jnp.float32,
            )
            part = more if part is None else part + more
        out_ref[:, at * half_in : (at + 1) * half_in] = part.astype(jnp.bfloat16)


def patch_gradient(grad, pieces, width_in):
    rows, model = grad.shape
    shards = pieces.shape[1]
    half_in = width_in // shards // 2
    return pl.pallas_call(
        functools.partial(patch_kernel, half_in),
        grid=(shards,),
        in_specs=[
            pl.BlockSpec((rows, model), lambda i: (0, 0)),
            pl.BlockSpec((GROUPS, 1, *pieces.shape[2:]), lambda i: (0, i, 0, 0)),
        ],
        out_specs=pl.BlockSpec((rows, 2 * half_in), lambda i: (0, i)),
        out_shape=jax.ShapeDtypeStruct((rows, width_in), jnp.bfloat16),
        name="patch_gradient",
    )(grad, pieces)


def mlp_kernel(
    order_ref, low_ref, tangent_ref, weight_ref, bias_ref,
    lowered_ref, back_ref, given_ref, first_ref, second_ref, dbias_ref, turned,
):
    step = pl.program_id(0)
    shards, _, model = weight_ref.shape[1:]
    unit = model // shards
    up = weight_ref[0, :, :unit, :].reshape(model, model)
    down = weight_ref[0, :, unit : 2 * unit, :].reshape(model, model)
    tangent = tangent_ref[...]

    @pl.when(step == 0)
    def _():
        turned[...] = low_ref[...].T

    upper = jnp.dot(low_ref[...], up, preferred_element_type=jnp.float32) + bias_ref[0]
    value, slope = gelu_parts(upper)
    gate = value.astype(jnp.bfloat16)
    lowered = jnp.dot(gate, down, preferred_element_type=jnp.float32)
    gate_grad = lax.dot_general(
        tangent, down, (((1,), (1,)), ((), ())), preferred_element_type=jnp.float32
    )
    upper_grad = (gate_grad * slope).astype(jnp.bfloat16)
    back = lax.dot_general(
        upper_grad, up, (((1,), (1,)), ((), ())), preferred_element_type=jnp.float32
    )
    dup = jnp.dot(turned[...], upper_grad, preferred_element_type=jnp.float32)
    ddown = jnp.dot(gate.T, tangent, preferred_element_type=jnp.float32)
    dup = dup.astype(jnp.bfloat16).reshape(shards, unit, model)
    ddown = ddown.astype(jnp.bfloat16).reshape(shards, unit, model)
    dbias_ref[0] = jnp.sum(upper_grad.astype(jnp.float32), axis=0, keepdims=True)

    @pl.when(step < 2)
    def _():
        given_ref[0, :, :unit, :] = dup
        given_ref[0, :, unit:, :] = ddown

    @pl.when(step == 2)
    def _():
        first_ref[:, :unit, :] = dup
        first_ref[:, unit:, :] = ddown

    @pl.when(step == 3)
    def _():
        second_ref[:, :unit, :] = dup
        second_ref[:, unit:, :] = ddown

    @pl.when(step == 0)
    def _():
        lowered_ref[...] = lowered
        back_ref[...] = back

    @pl.when(step > 0)
    def _():
        lowered_ref[...] += lowered
        back_ref[...] += back


def mlp(order, low, tangent, weights, bias):
    rows, model = low.shape
    _, shards, packed, _ = weights.shape
    both = 2 * (model // shards)
    resident = pl.BlockSpec((rows, model), lambda i, o: (0, 0))
    small = pl.BlockSpec((1, 1, model), lambda i, o: (o[i], 0, 0))
    kept = pl.BlockSpec((shards, both, model), lambda i, o: (0, 0, 0))
    return pl.pallas_call(
        mlp_kernel,
        grid_spec=pltpu.PrefetchScalarGridSpec(
            num_scalar_prefetch=1,
            grid=(GROUPS,),
            in_specs=[
                resident,
                resident,
                pl.BlockSpec((1, shards, packed, model), lambda i, o: (o[i], 0, 0, 0)),
                small,
            ],
            out_specs=[
                resident,
                resident,
                pl.BlockSpec((1, shards, both, model), lambda i, o: (jnp.minimum(i, 1), 0, 0, 0)),
                kept,
                kept,
                small,
            ],
            scratch_shapes=[pltpu.VMEM((model, rows), jnp.bfloat16)],
        ),
        out_shape=[
            jax.ShapeDtypeStruct((rows, model), jnp.float32),
            jax.ShapeDtypeStruct((rows, model), jnp.float32),
            jax.ShapeDtypeStruct((2, shards, both, model), jnp.bfloat16),
            jax.ShapeDtypeStruct((shards, both, model), jnp.bfloat16),
            jax.ShapeDtypeStruct((shards, both, model), jnp.bfloat16),
            jax.ShapeDtypeStruct((GROUPS, 1, model), jnp.float32),
        ],
        name="mlp",
    )(order, low, tangent, weights, bias)


def norm_forward(values, gain, shift):
    center = values - jnp.mean(values, axis=-1, keepdims=True)
    inverse = lax.rsqrt(jnp.mean(center * center, axis=-1, keepdims=True) + EPS)
    scaled = center * inverse
    return (scaled * gain + shift).astype(jnp.bfloat16), scaled, inverse


def norm_backward(grad, scaled, inverse, gain):
    inner = grad * gain
    back = inverse * (
        inner
        - jnp.mean(inner, axis=-1, keepdims=True)
        - scaled * jnp.mean(inner * scaled, axis=-1, keepdims=True)
    )
    return back, jnp.sum(grad * scaled, axis=0), jnp.sum(grad, axis=0)


def per_device(groups_dp, shards, *arguments):
    (
        patches, embedding, first_gain, first_shift, joint_weight, output_weight,
        second_gain, second_shift, up_weight, up_bias, down_weight, down_bias,
        block_number, cotangent,
    ) = arguments
    f32, bf16 = jnp.float32, jnp.bfloat16
    _, rows, width_in = patches.shape
    model = output_weight.shape[1]
    half = model // 2
    unit = model // shards
    hidden_units = up_weight.shape[1]
    piece = hidden_units // (GROUPS * shards)
    embed_rows = embedding.shape[0]
    width = shards // GROUPS
    feature = model // GROUPS
    fast = groups_dp == 4 and shards == 8
    dp, seq = lax.axis_index("dp"), lax.axis_index("seq")
    own_group, own_part = seq // width, seq % width
    core = dp % 2 if fast else jnp.int32(0)
    chip = dp // 2 if fast else jnp.int32(0)

    everyone = [(d, s) for d in range(groups_dp) for s in range(shards)]

    def moved(value, rule):
        pairs = []
        for d, s in everyone:
            there = rule(d, s)
            pairs.append((d * shards + s, there[0] * shards + there[1]))
        return lax.ppermute(value, AXES, pairs)

    def along_groups(value, by):
        return moved(value, lambda d, s: (d, ((s // width + by) % GROUPS) * width + s % width))

    def along_parts(value, by):
        return moved(value, lambda d, s: (d, (s // width) * width + (s % width + by) % width))

    def to_core(value):
        return moved(value, lambda d, s: (d ^ 1, s))

    def to_chip(value):
        return moved(value, lambda d, s: (d ^ 2, s))

    def at_index(value, at):
        return lax.dynamic_index_in_dim(value, at, 0, keepdims=False)

    def gathered(quarters):
        if fast:
            mine = at_index(quarters, dp)
            whole = lax.all_gather(mine, AXES, axis=0, tiled=False)
            return whole.reshape(GROUPS, shards, *mine.shape)
        whole = lax.all_gather(quarters, "seq", axis=0, tiled=False)
        return jnp.swapaxes(whole, 0, 1)

    joint_quarters = jnp.transpose(joint_weight.reshape(unit, 3, GROUPS, feature), (2, 0, 1, 3)).reshape(
        GROUPS, unit, 3 * feature
    )
    embed_quarters = jnp.transpose(
        embedding.reshape(2, embed_rows // 2, 2, half), (0, 2, 1, 3)
    ).reshape(GROUPS, embed_rows // 2, half)
    last = joint_quarters[:, :, half:].reshape(GROUPS, 2, unit // 2, feature)
    pieces = gathered(
        jnp.concatenate(
            [embed_quarters, joint_quarters[:, :, :half], jnp.concatenate([last[:, 0], last[:, 1]], axis=-1)],
            axis=1,
        )
    )
    up_quarters = jnp.transpose(
        up_weight.reshape(unit, shards, GROUPS, piece), (2, 0, 1, 3)
    ).reshape(GROUPS, unit, model)
    later = gathered(
        jnp.concatenate(
            [
                up_quarters,
                down_weight.reshape(GROUPS, piece, model),
                output_weight.reshape(GROUPS, unit // GROUPS, model),
            ],
            axis=1,
        )
    )
    output_full = jnp.swapaxes(later[:, :, 2 * unit :], 0, 1).reshape(model, model)

    vectors = jnp.concatenate([first_gain, first_shift, second_gain, second_shift, down_bias, up_bias])
    count = vectors.shape[0]
    if fast:
        spread = jnp.where(jnp.arange(shards)[:, None] == seq, vectors[None], jnp.zeros((), bf16))
        for bit in (1, 2, 4):
            spread = spread + moved(spread, lambda d, s, bit=bit: (d, s ^ bit))
    else:
        spread = lax.all_gather(vectors, "seq", axis=0, tiled=False)
    vector_all = spread.astype(f32)
    gain_one, shift_one, gain_two, shift_two, bias_down = (
        vector_all[:, at * unit : (at + 1) * unit].reshape(1, model) for at in range(5)
    )
    bias_up = jnp.transpose(
        vector_all[:, 5 * unit :].reshape(shards, GROUPS, piece), (1, 0, 2)
    ).reshape(GROUPS, 1, model)

    ids = block_number[0]
    ends = jnp.sum((ids[None, :] <= ids[:, None]).astype(jnp.int32), axis=1)
    ends = ends.reshape(shards, 1, rows)
    place = jnp.concatenate([jnp.stack([own_group, own_part]).astype(jnp.int32), ends[:, 0, -1]])

    flat_in = patches[0]
    tangent = cotangent[0]
    hidden, normed1, joint, joint_full = embed(flat_in, pieces, gain_one, shift_one, unit)

    def scattered(value):
        got = [at_index(value, own_group)]
        for by in range(1, GROUPS):
            got.append(along_groups(at_index(value, (own_group + by) % GROUPS), by))
        return got

    def returned(parts):
        whole = jnp.zeros((GROUPS, *parts[0].shape), parts[0].dtype)
        for by in range(GROUPS):
            part = parts[by] if by == 0 else along_groups(parts[by], GROUPS - by)
            whole = lax.dynamic_update_index_in_dim(whole, part, (own_group + by) % GROUPS, 0)
        return whole

    arrived = scattered(joint)
    halves = [part[feature:] for part in arrived]
    every_pair = [jnp.stack(halves)]
    for by in range(1, width):
        every_pair.append(jnp.stack([along_parts(part, by) for part in halves]))
    pairs = jnp.stack(every_pair).reshape(width, GROUPS, 2, PER, HEAD_DIM, rows)
    query = jnp.stack([part[:feature] for part in arrived]).reshape(GROUPS, PER, HEAD_DIM, rows)
    out, logs = attention_forward(place, query, pairs, ends)
    flat_out = out.reshape(GROUPS, feature, rows)
    attended = returned([flat_out[by] for by in range(GROUPS)]).reshape(model, rows)

    resid = hidden + lax.dot_general(
        attended, output_full, (((0,), (0,)), ((), ())), preferred_element_type=f32
    )
    normed2, scaled2, inverse2 = norm_forward(resid, gain_two, shift_two)
    order = jnp.stack(
        [(1 - chip) * 2 + 1 - core, chip * 2 + 1 - core, (1 - chip) * 2 + core, chip * 2 + core]
    ).astype(jnp.int32)
    lowered, normed2_grad, given, kept_far, kept_near, bias_up_grad = mlp(order, normed2, tangent, later, bias_up)
    block_output = (resid + lowered + bias_down).astype(bf16)[None]

    def added(*terms):
        total = terms[0].astype(f32)
        for term in terms[1:]:
            total = total + term.astype(f32)
        return total.astype(bf16)

    def scatter(value):
        return lax.psum_scatter(value, "seq", scatter_dimension=0, tiled=False)

    def slow(value):
        return lax.psum(scatter(value), "dp")

    if fast:
        swapped = to_core(given)
        far = added(kept_far, swapped[0])
        near = added(kept_near, swapped[1], to_chip(far))
        group_own = scatter(near)
        group_far = to_chip(group_own)
        pair_own = jnp.stack([group_own, group_far])
        pair_other = to_core(pair_own)
        mlp_shard = jnp.zeros((GROUPS, *group_own.shape), bf16)
        for at, value in ((3, pair_own[0]), (2, pair_own[1]), (1, pair_other[0]), (0, pair_other[1])):
            mlp_shard = lax.dynamic_update_index_in_dim(mlp_shard, value, order[at], 0)
    else:
        mlp_shard = jnp.stack([slow(kept_near), slow(given[1]), slow(kept_far), slow(given[0])])
    mlp_shard = mlp_shard.astype(f32)
    up_grad = jnp.transpose(
        mlp_shard[:, :unit].reshape(GROUPS, unit, shards, piece), (1, 2, 0, 3)
    ).reshape(unit, hidden_units)
    down_grad = mlp_shard[:, unit:].reshape(GROUPS * piece, model)

    def reduced(make):
        if not fast:
            return slow(make(0).astype(bf16)).astype(f32), slow(make(1).astype(bf16)).astype(f32)
        swapped = to_core(make(1 - core).astype(bf16))
        both = (make(core) + swapped.astype(f32)).astype(bf16)
        mine = scatter(both)
        mine = added(mine, to_chip(mine))
        other = to_core(mine)
        pick = core == 0
        return (
            jnp.where(pick, mine, other).astype(f32),
            jnp.where(pick, other, mine).astype(f32),
        )

    def columns(value, side):
        return lax.dynamic_slice_in_dim(value, side * half, half, 1)

    tangent_wide = tangent.astype(f32)
    resid_back, gain_two_grad, shift_two_grad = norm_backward(normed2_grad, scaled2, inverse2, gain_two)
    resid_grad = tangent_wide + resid_back
    mixed_grad = resid_grad.astype(bf16)
    attended_grad = lax.dot_general(
        output_full, mixed_grad, (((1,), (1,)), ((), ())), preferred_element_type=f32
    ).astype(bf16)
    grad_in = jnp.stack(scattered(attended_grad.reshape(GROUPS, feature, rows)))
    grad_in = grad_in.reshape(GROUPS, PER, HEAD_DIM, rows)
    dquery, dpairs = attention_backward(place, query, pairs, ends, logs, out, grad_in)
    dpair_own = dpairs[0].reshape(GROUPS, 2 * feature, rows)
    for by in range(1, width):
        dpair_own = added(dpair_own, along_parts(dpairs[by].reshape(GROUPS, 2 * feature, rows), width - by))
    joint_back = jnp.concatenate([dquery.reshape(GROUPS, feature, rows), dpair_own], axis=1)
    joint_grad = returned([joint_back[by] for by in range(GROUPS)])

    output_halves = reduced(
        lambda side: jnp.dot(attended, columns(mixed_grad, side), preferred_element_type=f32).reshape(
            shards, unit, half
        )
    )
    output_shard = jnp.concatenate(output_halves, axis=-1)

    def joint_half(side):
        part = lax.dynamic_slice_in_dim(joint_grad, 2 * side, 2, 0).reshape(6 * feature, rows)
        return lax.dot_general(
            normed1, part, (((0,), (1,)), ((), ())), preferred_element_type=f32
        ).reshape(shards, unit, 6 * feature)

    joint_shard = jnp.stack(reduced(joint_half), axis=1).reshape(unit, GROUPS, 3, feature)
    joint_shard = jnp.swapaxes(joint_shard, 1, 2).reshape(unit, 3 * model)

    normed1_grad = jnp.einsum("gnr,gkn->rk", joint_grad, joint_full, preferred_element_type=f32)
    _, scaled1, inverse1 = norm_forward(hidden, gain_one, shift_one)
    hidden_back, gain_one_grad, shift_one_grad = norm_backward(normed1_grad, scaled1, inverse1, gain_one)
    hidden_grad = (resid_grad + hidden_back).astype(bf16)
    embed_halves = reduced(
        lambda side: lax.dot_general(
            flat_in, columns(hidden_grad, side), (((0,), (0,)), ((), ())), preferred_element_type=f32
        ).reshape(shards, embed_rows, half)
    )
    embed_shard = jnp.concatenate(embed_halves, axis=-1)
    patches_grad = patch_gradient(hidden_grad, pieces, width_in)[None]

    tangent_sum = jnp.sum(tangent_wide, axis=0)
    bias_up_natural = jnp.transpose(bias_up_grad.reshape(GROUPS, shards, piece), (1, 0, 2))
    packed = jnp.concatenate(
        [
            part.reshape(shards, -1)
            for part in (gain_one_grad, shift_one_grad, gain_two_grad, shift_two_grad, tangent_sum, bias_up_natural)
        ],
        axis=1,
    )
    if fast:
        packed = packed + to_core(packed)
        packed = packed + to_chip(packed)
        for bit in (1, 2, 4):
            packed = packed + moved(packed, lambda d, s, bit=bit: (d, s ^ bit))
    else:
        packed = lax.psum(packed, AXES)
    own_vectors = at_index(packed, seq)
    own = [own_vectors[at * unit : (at + 1) * unit] for at in range(5)]
    return (
        block_output,
        patches_grad,
        embed_shard,
        own[0],
        own[1],
        joint_shard,
        output_shard,
        own[2],
        own[3],
        up_grad,
        own_vectors[5 * unit :],
        down_grad,
        own[4],
    )


def solution(mesh):
    rows, columns, vector = P("dp", "seq", None), P("seq", None), P("seq")
    placed = (
        rows, columns, vector, vector, columns, columns, vector, vector,
        columns, vector, columns, vector, P("dp", None), rows,
    )
    given = (
        rows, rows, columns, vector, vector, columns, columns,
        vector, vector, columns, vector, columns, vector,
    )
    return jax.shard_map(
        functools.partial(per_device, mesh.shape["dp"], mesh.shape["seq"]),
        mesh=mesh,
        in_specs=placed,
        out_specs=given,
        check_vma=False,
    )
```

```python
import functools
import math

import jax
import jax.numpy as jnp
from jax import lax
from jax.experimental import pallas as pl
from jax.experimental.pallas import tpu as pltpu
from jax.sharding import PartitionSpec as P

AXES = ("dp", "seq")
EPS = 1e-05
HEAD_DIM = 64
GROUPS = 4
PER = 3
EDGE = 256
NEG = -1e30
SCALE = HEAD_DIM ** (-0.5)
LOG2E = math.log2(math.e)
SCALE2 = SCALE * LOG2E


def slot_of(place_ref, part, width):
    own_group, own_part = place_ref[0], place_ref[1]
    group, inner = part // width, part % width
    return (own_part - inner + width) % width * GROUPS + (own_group - group + GROUPS) % GROUPS


def spent(micros):
    return pl.CostEstimate(flops=micros * 10**9, bytes_accessed=0, transcendentals=0)


def whole_block(shape):
    return pl.BlockSpec(shape, lambda *_: (0,) * len(shape))


def at_step(step, refs, use):
    for at, ref in enumerate(refs):

        @pl.when(step == at)
        def _(ref=ref):
            use(ref)


def fill_slots(parts, others, use):
    for by, part in enumerate(parts):
        use(by, part[1], part[2])
    for inner, other in enumerate(others):
        for by in range(GROUPS):
            use((inner + 1) * GROUPS + by, other[by, 0], other[by, 1])


def forward_kernel(width, place_ref, ends_ref, *refs):
    parts_in, others = refs[:GROUPS], refs[GROUPS : GROUPS + width - 1]
    outs, log_ref = refs[GROUPS + width - 1 : -7], refs[-7]
    keys, values, query, top, total, accum = refs[-6:]
    step = pl.program_id(0)
    rows = query.shape[-1]
    parts = width * GROUPS

    @pl.when(step == 0)
    def _():
        def use(slot, key, value):
            keys[slot] = key.T
            values[slot] = value

        fill_slots(parts_in, others, use)

    def take(ref):
        query[...] = ref[0]

    at_step(step, parts_in, take)
    own = ((place_ref[0] - step + GROUPS) % GROUPS) * width + place_ref[1]

    def tile(part, kspan, qspan, masked, first):
        slot = slot_of(place_ref, part, width)
        k0, kn = kspan
        q0, qn = qspan
        scores = jnp.dot(
            keys[slot, k0 : k0 + kn, :], query[:, q0 : q0 + qn], preferred_element_type=jnp.float32
        )
        if masked:
            at = part * rows + k0 + lax.broadcasted_iota(jnp.int32, (kn, qn), 0)
            scores = jnp.where(at < ends_ref[own, :, q0 : q0 + qn], scores, NEG)
        new_top = jnp.max(scores, axis=0, keepdims=True) * SCALE2
        if not first:
            old_top = top[:, q0 : q0 + qn]
            new_top = jnp.maximum(old_top, new_top)
        weights = jnp.exp2(scores * SCALE2 - new_top)
        added = jnp.sum(weights, axis=0, keepdims=True)
        mixed = jnp.dot(
            values[slot, :, k0 : k0 + kn], weights.astype(jnp.bfloat16), preferred_element_type=jnp.float32
        )
        if first:
            total[:, q0 : q0 + qn] = added
            accum[:, q0 : q0 + qn] = mixed
        else:
            shrink = jnp.exp2(old_top - new_top)
            total[:, q0 : q0 + qn] = total[:, q0 : q0 + qn] * shrink + added
            accum[:, q0 : q0 + qn] = accum[:, q0 : q0 + qn] * shrink + mixed
        top[:, q0 : q0 + qn] = new_top

    tile(own, (0, rows), (0, rows), True, True)

    @pl.when(jnp.logical_and(own + 1 < parts, place_ref[2 + own] > (own + 1) * rows))
    def _():
        tile(own + 1, (0, EDGE), (rows - EDGE, EDGE), True, False)

    def whole(part, carry):
        tile(part, (0, rows), (0, rows), False, False)
        return carry

    lax.fori_loop(0, own, whole, 0)
    result = (accum[...] / total[...]).astype(jnp.bfloat16)

    def give(ref):
        ref[...] = result

    at_step(step, outs, give)
    log_ref[0] = top[...] + jnp.log2(total[...])


def attention_forward(place, ends, parts_in, others):
    width, rows = len(others) + 1, parts_in[0].shape[-1]
    parts = width * GROUPS
    return pl.pallas_call(
        functools.partial(forward_kernel, width),
        grid_spec=pltpu.PrefetchScalarGridSpec(
            num_scalar_prefetch=1,
            grid=(GROUPS,),
            in_specs=[whole_block(value.shape) for value in (ends, *parts_in, *others)],
            out_specs=[whole_block((HEAD_DIM, rows))] * GROUPS
            + [pl.BlockSpec((1, 1, rows), lambda i, p: (i, 0, 0))],
            scratch_shapes=[
                pltpu.VMEM((parts, rows, HEAD_DIM), jnp.bfloat16),
                pltpu.VMEM((parts, HEAD_DIM, rows), jnp.bfloat16),
                pltpu.VMEM((HEAD_DIM, rows), jnp.bfloat16),
                pltpu.VMEM((1, rows), jnp.float32),
                pltpu.VMEM((1, rows), jnp.float32),
                pltpu.VMEM((HEAD_DIM, rows), jnp.float32),
            ],
        ),
        out_shape=[jax.ShapeDtypeStruct((HEAD_DIM, rows), jnp.bfloat16)] * GROUPS
        + [jax.ShapeDtypeStruct((GROUPS, 1, rows), jnp.float32)],
        cost_estimate=spent(17),
        name="attention_forward",
    )(place, ends, *parts_in, *others)


def pack_kernel(*refs):
    for by, ref in enumerate(refs[:-1]):
        refs[-1][by] = ref[1:]


def pack(parts_in):
    rows = parts_in[0].shape[-1]
    return pl.pallas_call(
        pack_kernel,
        out_shape=jax.ShapeDtypeStruct((GROUPS, 2, HEAD_DIM, rows), jnp.bfloat16),
        cost_estimate=spent(1),
        name="pack",
    )(*parts_in)


def merge_kernel(width, *refs):
    near, others, outs = refs[0], refs[1:width], refs[width:]
    for by, out in enumerate(outs):
        out[0] = near[by, 0]
        total = near[by, 1:].astype(jnp.float32)
        for other in others:
            total = total + other[by].astype(jnp.float32)
        out[1:] = total.astype(jnp.bfloat16)


def merge(near, others):
    return pl.pallas_call(
        functools.partial(merge_kernel, len(others) + 1),
        out_shape=[jax.ShapeDtypeStruct(near.shape[1:], jnp.bfloat16)] * GROUPS,
        cost_estimate=spent(2),
        name="merge",
    )(near, *others)


def backward_kernel(width, place_ref, ends_ref, log_ref, *refs):
    parts_in, others = refs[:GROUPS], refs[GROUPS : GROUPS + width - 1]
    refs = refs[GROUPS + width - 1 :]
    outs, grads, near_ref, far_refs = refs[:GROUPS], refs[GROUPS : 2 * GROUPS], refs[8], refs[9 : 8 + width]
    keys, keys_raw, values, dkeys, dvalues, query, grad, query_turned, grad_turned, delta, dquery = refs[8 + width :]
    step = pl.program_id(0)
    rows = query.shape[-1]
    parts = width * GROUPS

    @pl.when(step == 0)
    def _():
        def use(slot, key, value):
            keys[slot] = key.T
            keys_raw[slot] = key
            values[slot] = value.T
            dkeys[slot] = jnp.zeros((rows, HEAD_DIM), jnp.float32)
            dvalues[slot] = jnp.zeros((rows, HEAD_DIM), jnp.float32)

        fill_slots(parts_in, others, use)

    for at in range(GROUPS):

        @pl.when(step == at)
        def _(at=at):
            query[...] = parts_in[at][0]
            grad[...] = grads[at][...]
            delta[...] = jnp.sum(
                grads[at][...].astype(jnp.float32) * outs[at][...].astype(jnp.float32), axis=0, keepdims=True
            )

    query_turned[...] = query[...].T
    grad_turned[...] = grad[...].T
    dquery[...] = jnp.zeros((HEAD_DIM, rows), jnp.float32)
    own = ((place_ref[0] - step + GROUPS) % GROUPS) * width + place_ref[1]

    def tile(part, kspan, qspan, masked):
        slot = slot_of(place_ref, part, width)
        k0, kn = kspan
        for q0 in range(qspan[0], qspan[0] + qspan[1], EDGE):
            qn = EDGE
            scores = jnp.dot(
                keys[slot, k0 : k0 + kn, :], query[:, q0 : q0 + qn], preferred_element_type=jnp.float32
            )
            if masked:
                at = part * rows + k0 + lax.broadcasted_iota(jnp.int32, (kn, qn), 0)
                scores = jnp.where(at < ends_ref[own, :, q0 : q0 + qn], scores, NEG)
            weights = jnp.exp2(scores * SCALE2 - log_ref[0, :, q0 : q0 + qn])
            dweights = jnp.dot(
                values[slot, k0 : k0 + kn, :], grad[:, q0 : q0 + qn], preferred_element_type=jnp.float32
            )
            dscores = (weights * (dweights - delta[:, q0 : q0 + qn])).astype(jnp.bfloat16)
            dvalues[slot, k0 : k0 + kn, :] += jnp.dot(
                weights.astype(jnp.bfloat16), grad_turned[q0 : q0 + qn, :], preferred_element_type=jnp.float32
            )
            dkeys[slot, k0 : k0 + kn, :] += jnp.dot(
                dscores, query_turned[q0 : q0 + qn, :], preferred_element_type=jnp.float32
            )
            dquery[:, q0 : q0 + qn] += jnp.dot(
                keys_raw[slot, :, k0 : k0 + kn], dscores, preferred_element_type=jnp.float32
            )

    tile(own, (0, rows), (0, rows), True)

    @pl.when(jnp.logical_and(own + 1 < parts, place_ref[2 + own] > (own + 1) * rows))
    def _():
        tile(own + 1, (0, EDGE), (rows - EDGE, EDGE), True)

    def whole(part, carry):
        tile(part, (0, rows), (0, rows), False)
        return carry

    lax.fori_loop(0, own, whole, 0)
    near_ref[step, 0] = (dquery[...] * SCALE).astype(jnp.bfloat16)

    @pl.when(step == GROUPS - 1)
    def _():
        for slot in range(parts):
            inner, by = slot // GROUPS, slot % GROUPS
            ref, base = (near_ref, 1) if inner == 0 else (far_refs[inner - 1], 0)
            ref[by, base] = (dkeys[slot] * SCALE).T.astype(jnp.bfloat16)
            ref[by, base + 1] = dvalues[slot].T.astype(jnp.bfloat16)


def attention_backward(place, ends, logs, parts_in, others, outs, grads):
    width, rows = len(others) + 1, parts_in[0].shape[-1]
    parts = width * GROUPS
    shapes = [(GROUPS, 3, HEAD_DIM, rows)] + [(GROUPS, 2, HEAD_DIM, rows)] * (width - 1)
    turned = (rows, HEAD_DIM)
    return pl.pallas_call(
        functools.partial(backward_kernel, width),
        grid_spec=pltpu.PrefetchScalarGridSpec(
            num_scalar_prefetch=1,
            grid=(GROUPS,),
            in_specs=[whole_block(ends.shape), pl.BlockSpec((1, 1, rows), lambda i, p: (i, 0, 0))]
            + [whole_block(value.shape) for value in (*parts_in, *others, *outs, *grads)],
            out_specs=[whole_block(shape) for shape in shapes],
            scratch_shapes=[
                pltpu.VMEM((parts, *turned), jnp.bfloat16),
                pltpu.VMEM((parts, HEAD_DIM, rows), jnp.bfloat16),
                pltpu.VMEM((parts, *turned), jnp.bfloat16),
                pltpu.VMEM((parts, *turned), jnp.float32),
                pltpu.VMEM((parts, *turned), jnp.float32),
                pltpu.VMEM((HEAD_DIM, rows), jnp.bfloat16),
                pltpu.VMEM((HEAD_DIM, rows), jnp.bfloat16),
                pltpu.VMEM(turned, jnp.bfloat16),
                pltpu.VMEM(turned, jnp.bfloat16),
                pltpu.VMEM((1, rows), jnp.float32),
                pltpu.VMEM((HEAD_DIM, rows), jnp.float32),
            ],
        ),
        out_shape=[jax.ShapeDtypeStruct(shape, jnp.bfloat16) for shape in shapes],
        cost_estimate=spent(21),
        name="attention_backward",
    )(place, ends, logs, *parts_in, *others, *outs, *grads)


def whole_call(kernel, name, micros, scalars, values, shapes, scratch=()):
    return pl.pallas_call(
        kernel,
        grid_spec=pltpu.PrefetchScalarGridSpec(
            num_scalar_prefetch=1,
            grid=(1,),
            in_specs=[whole_block(value.shape) for value in values],
            out_specs=[whole_block(shape) for shape, _ in shapes],
            scratch_shapes=list(scratch),
        ),
        out_shape=[jax.ShapeDtypeStruct(shape, kind) for shape, kind in shapes],
        cost_estimate=spent(micros),
        name=name,
    )(scalars, *values)


def resid_kernel(place_ref, hidden_ref, weight_ref, gain_ref, shift_ref, *refs):
    parts, resid_ref, normed_ref, attended_ref = refs[:-3], *refs[-3:]
    for by in range(GROUPS):
        group = (place_ref[0] + by) % GROUPS
        for head in range(PER):
            attended_ref[group, head * HEAD_DIM : (head + 1) * HEAD_DIM] = parts[by * PER + head][...]
    resid = hidden_ref[...]
    for group in range(GROUPS):
        resid = resid + lax.dot_general(
            attended_ref[group], weight_ref[group], (((0,), (0,)), ((), ())), preferred_element_type=jnp.float32
        )
    resid_ref[...] = resid
    normed_ref[...] = norm_forward(resid, gain_ref[...], shift_ref[...])[0]


def mixed_kernel(
    place_ref, resid_ref, lowered_ref, bias_ref, back_ref, tangent_ref, gain_ref, shift_ref, weight_ref,
    output_ref, grad_ref, mixed_ref, sums_ref, *parts,
):
    resid = resid_ref[...]
    output_ref[...] = (resid + lowered_ref[...] + bias_ref[...]).astype(jnp.bfloat16)
    gain = gain_ref[...]
    _, scaled, inverse = norm_forward(resid, gain, shift_ref[...])
    back, gain_grad, shift_grad = norm_backward(back_ref[...], scaled, inverse, gain)
    tangent = tangent_ref[...].astype(jnp.float32)
    total = tangent + back
    grad_ref[...] = total
    mixed = total.astype(jnp.bfloat16)
    mixed_ref[...] = mixed
    sums_ref[0:1] = gain_grad
    sums_ref[1:2] = shift_grad
    sums_ref[2:3] = jnp.sum(tangent, axis=0, keepdims=True)
    for by in range(GROUPS):
        part = lax.dot_general(
            weight_ref[(place_ref[0] + by) % GROUPS],
            mixed,
            (((1,), (1,)), ((), ())),
            preferred_element_type=jnp.float32,
        ).astype(jnp.bfloat16)
        for head in range(PER):
            parts[by * PER + head][...] = part[head * HEAD_DIM : (head + 1) * HEAD_DIM]


def hidden_kernel(
    place_ref, weight_ref, hidden_ref, gain_ref, shift_ref, resid_ref, *refs
):
    parts, joint_ref, grad_ref, given_ref, kept_ref, sums_ref = refs[:-5], *refs[-5:]
    for by in range(GROUPS):
        group = (place_ref[0] + by) % GROUPS
        for head in range(PER):
            for kind in range(3):
                at = (kind * PER + head) * HEAD_DIM
                joint_ref[group, at : at + HEAD_DIM] = parts[by * PER + head][kind]
    back = None
    for group in range(GROUPS):
        more = lax.dot_general(
            joint_ref[group], weight_ref[group], (((0,), (1,)), ((), ())), preferred_element_type=jnp.float32
        )
        back = more if back is None else back + more
    gain = gain_ref[...]
    _, scaled, inverse = norm_forward(hidden_ref[...], gain, shift_ref[...])
    back, gain_grad, shift_grad = norm_backward(back, scaled, inverse, gain)
    grad = (resid_ref[...] + back).astype(jnp.bfloat16)
    grad_ref[...] = grad
    sums_ref[0:1] = gain_grad
    sums_ref[1:2] = shift_grad
    turned = grad.T
    half = turned.shape[0] // 2
    core = place_ref[2]

    @pl.when(core == 0)
    def _():
        given_ref[...] = turned[half:]
        kept_ref[...] = turned[:half]

    @pl.when(core != 0)
    def _():
        given_ref[...] = turned[:half]
        kept_ref[...] = turned[half:]


def embed_gradient_kernel(patches_ref, turned_ref, out_ref):
    out_ref[0] = jnp.dot(turned_ref[...], patches_ref[...], preferred_element_type=jnp.float32).astype(jnp.bfloat16)


def embed_gradient(patches, turned, shards):
    rows, width_in = patches.shape
    half, each = turned.shape[0], width_in // shards
    return pl.pallas_call(
        embed_gradient_kernel,
        grid=(shards,),
        in_specs=[pl.BlockSpec((rows, each), lambda i: (0, i)), whole_block(turned.shape)],
        out_specs=pl.BlockSpec((1, half, each), lambda i: (i, 0, 0)),
        out_shape=jax.ShapeDtypeStruct((shards, half, each), jnp.bfloat16),
        cost_estimate=spent(5),
        name="embed_gradient",
    )(patches, turned)


def square_kernel(side_ref, normed_ref, joint_ref, attended_ref, mixed_ref, out):
    turned = normed_ref[...].T
    shards, blocks, unit, half = out.shape
    wide, side = joint_ref.shape[1], side_ref[0]
    both = joint_ref[pl.ds(2 * side, 2)].reshape(2 * wide, joint_ref.shape[2])
    for at in range(blocks - 1):
        part = lax.dot_general(
            turned, both[at * half : (at + 1) * half], (((1,), (1,)), ((), ())),
            preferred_element_type=jnp.float32,
        )
        out[:, at] = part.astype(jnp.bfloat16).reshape(shards, unit, half)
    columns = mixed_ref[:, pl.ds(pl.multiple_of(side * half, half), half)]
    part = jnp.dot(attended_ref[...], columns, preferred_element_type=jnp.float32)
    out[:, blocks - 1] = part.astype(jnp.bfloat16).reshape(shards, unit, half)


def gelu_parts(upper):
    inner = math.sqrt(2 / math.pi) * (upper + 0.044715 * upper * upper * upper)
    bent = jnp.tanh(inner)
    value = 0.5 * upper * (1 + bent)
    slope = 0.5 * (1 + bent) + 0.5 * upper * (1 - bent * bent) * math.sqrt(2 / math.pi) * (
        1 + 3 * 0.044715 * upper * upper
    )
    return value, slope


def embed_kernel(
    sizes, place_ref, patches_ref, pieces_ref, gain_ref, shift_ref, hidden_ref, normed_ref, full_ref, *joint_refs
):
    step = pl.program_id(0)
    half_in, unit = sizes
    wide = pieces_ref.shape[-1]
    third = wide // 2
    parts = []
    for side in range(2):
        part = None
        for at in range(2):
            more = jnp.dot(
                patches_ref[:, at * half_in : (at + 1) * half_in],
                pieces_ref[at * 2 + side, 0, :half_in, :],
                preferred_element_type=jnp.float32,
            )
            part = more if part is None else part + more
        parts.append(part)
    for group in range(GROUPS):
        base = pl.multiple_of(step * unit, unit)
        middle = half_in + unit
        full_ref[group, pl.ds(base, unit), :wide] = pieces_ref[group, 0, half_in:middle, :]
        last = pieces_ref[group, 0, middle : middle + unit // 2, :]
        full_ref[group, pl.ds(base, unit // 2), wide:] = last[:, :third]
        full_ref[group, pl.ds(base + unit // 2, unit // 2), wide:] = last[:, third:]

    @pl.when(step == 0)
    def _():
        for side in range(2):
            hidden_ref[:, side * wide : (side + 1) * wide] = parts[side]

    @pl.when(step > 0)
    def _():
        for side in range(2):
            hidden_ref[:, side * wide : (side + 1) * wide] += parts[side]

    @pl.when(step == pl.num_programs(0) - 1)
    def _():
        normed = norm_forward(hidden_ref[...], gain_ref[...], shift_ref[...])[0]
        normed_ref[...] = normed
        for by in range(GROUPS):
            group = (place_ref[0] + by) % GROUPS
            turned = jnp.dot(normed, full_ref[group], preferred_element_type=jnp.float32).astype(jnp.bfloat16).T
            for head in range(PER):
                for kind in range(3):
                    at = (kind * PER + head) * HEAD_DIM
                    joint_refs[by * PER + head][kind] = turned[at : at + HEAD_DIM]


def embed(place, patches, pieces, gain, shift, unit):
    rows, width_in = patches.shape
    shards, model = pieces.shape[1], gain.shape[1]
    half_in = width_in // shards // 2
    wide = model // 2 * 3 // 2
    return pl.pallas_call(
        functools.partial(embed_kernel, (half_in, unit)),
        grid_spec=pltpu.PrefetchScalarGridSpec(
            num_scalar_prefetch=1,
            grid=(shards,),
            in_specs=[
                pl.BlockSpec((rows, 2 * half_in), lambda i, p: (0, i)),
                pl.BlockSpec((GROUPS, 1, *pieces.shape[2:]), lambda i, p: (0, i, 0, 0)),
                whole_block((1, model)),
                whole_block((1, model)),
            ],
            out_specs=[
                whole_block((rows, model)),
                whole_block((rows, model)),
                whole_block((GROUPS, model, wide)),
            ]
            + [whole_block((3, HEAD_DIM, rows))] * (GROUPS * PER),
        ),
        out_shape=[
            jax.ShapeDtypeStruct((rows, model), jnp.float32),
            jax.ShapeDtypeStruct((rows, model), jnp.bfloat16),
            jax.ShapeDtypeStruct((GROUPS, model, wide), jnp.bfloat16),
        ]
        + [jax.ShapeDtypeStruct((3, HEAD_DIM, rows), jnp.bfloat16)] * (GROUPS * PER),
        cost_estimate=spent(20),
        name="embed",
    )(place, patches, pieces, gain, shift)


def patch_kernel(half_in, grad_ref, pieces_ref, out_ref):
    wide = pieces_ref.shape[-1]
    for at in range(2):
        part = None
        for side in range(2):
            more = lax.dot_general(
                grad_ref[:, side * wide : (side + 1) * wide],
                pieces_ref[at * 2 + side, 0, :half_in, :],
                (((1,), (1,)), ((), ())),
                preferred_element_type=jnp.float32,
            )
            part = more if part is None else part + more
        out_ref[:, at * half_in : (at + 1) * half_in] = part.astype(jnp.bfloat16)


def patch_gradient(grad, pieces, width_in):
    rows, model = grad.shape
    shards = pieces.shape[1]
    half_in = width_in // shards // 2
    return pl.pallas_call(
        functools.partial(patch_kernel, half_in),
        grid=(shards,),
        in_specs=[
            pl.BlockSpec((rows, model), lambda i: (0, 0)),
            pl.BlockSpec((GROUPS, 1, *pieces.shape[2:]), lambda i: (0, i, 0, 0)),
        ],
        out_specs=pl.BlockSpec((rows, 2 * half_in), lambda i: (0, i)),
        out_shape=jax.ShapeDtypeStruct((rows, width_in), jnp.bfloat16),
        cost_estimate=spent(14),
        name="patch_gradient",
    )(grad, pieces)


def mlp_kernel(
    order_ref, low_ref, tangent_ref, weight_ref, bias_ref,
    lowered_ref, back_ref, given_ref, first_ref, second_ref, dbias_ref, turned,
):
    step = pl.program_id(0)
    shards, _, model = weight_ref.shape[1:]
    unit = model // shards
    up = weight_ref[0, :, :unit, :].reshape(model, model)
    down = weight_ref[0, :, unit : 2 * unit, :].reshape(model, model)
    tangent = tangent_ref[...]

    @pl.when(step == 0)
    def _():
        turned[...] = low_ref[...].T

    upper = jnp.dot(low_ref[...], up, preferred_element_type=jnp.float32) + bias_ref[0]
    value, slope = gelu_parts(upper)
    gate = value.astype(jnp.bfloat16)
    lowered = jnp.dot(gate, down, preferred_element_type=jnp.float32)
    gate_grad = lax.dot_general(
        tangent, down, (((1,), (1,)), ((), ())), preferred_element_type=jnp.float32
    )
    upper_grad = (gate_grad * slope).astype(jnp.bfloat16)
    back = lax.dot_general(
        upper_grad, up, (((1,), (1,)), ((), ())), preferred_element_type=jnp.float32
    )
    dup = jnp.dot(turned[...], upper_grad, preferred_element_type=jnp.float32)
    ddown = jnp.dot(gate.T, tangent, preferred_element_type=jnp.float32)
    dup = dup.astype(jnp.bfloat16).reshape(shards, unit, model)
    ddown = ddown.astype(jnp.bfloat16).reshape(shards, unit, model)
    dbias_ref[0] = jnp.sum(upper_grad.astype(jnp.float32), axis=0, keepdims=True)

    @pl.when(step < 2)
    def _():
        given_ref[0, :, :unit, :] = dup
        given_ref[0, :, unit:, :] = ddown

    @pl.when(step == 2)
    def _():
        first_ref[:, :unit, :] = dup
        first_ref[:, unit:, :] = ddown

    @pl.when(step == 3)
    def _():
        second_ref[:, :unit, :] = dup
        second_ref[:, unit:, :] = ddown

    @pl.when(step == 0)
    def _():
        lowered_ref[...] = lowered
        back_ref[...] = back

    @pl.when(step > 0)
    def _():
        lowered_ref[...] += lowered
        back_ref[...] += back


def mlp(order, low, tangent, weights, bias):
    rows, model = low.shape
    _, shards, packed, _ = weights.shape
    both = 2 * (model // shards)
    resident = pl.BlockSpec((rows, model), lambda i, o: (0, 0))
    small = pl.BlockSpec((1, 1, model), lambda i, o: (o[i], 0, 0))
    kept = pl.BlockSpec((shards, both, model), lambda i, o: (0, 0, 0))
    return pl.pallas_call(
        mlp_kernel,
        grid_spec=pltpu.PrefetchScalarGridSpec(
            num_scalar_prefetch=1,
            grid=(GROUPS,),
            in_specs=[
                resident,
                resident,
                pl.BlockSpec((1, shards, packed, model), lambda i, o: (o[i], 0, 0, 0)),
                small,
            ],
            out_specs=[
                resident,
                resident,
                pl.BlockSpec((1, shards, both, model), lambda i, o: (jnp.minimum(i, 1), 0, 0, 0)),
                kept,
                kept,
                small,
            ],
            scratch_shapes=[pltpu.VMEM((model, rows), jnp.bfloat16)],
        ),
        out_shape=[
            jax.ShapeDtypeStruct((rows, model), jnp.float32),
            jax.ShapeDtypeStruct((rows, model), jnp.float32),
            jax.ShapeDtypeStruct((2, shards, both, model), jnp.bfloat16),
            jax.ShapeDtypeStruct((shards, both, model), jnp.bfloat16),
            jax.ShapeDtypeStruct((shards, both, model), jnp.bfloat16),
            jax.ShapeDtypeStruct((GROUPS, 1, model), jnp.float32),
        ],
        cost_estimate=spent(28),
        name="mlp",
    )(order, low, tangent, weights, bias)


def norm_forward(values, gain, shift):
    center = values - jnp.mean(values, axis=-1, keepdims=True)
    inverse = lax.rsqrt(jnp.mean(center * center, axis=-1, keepdims=True) + EPS)
    scaled = center * inverse
    return (scaled * gain + shift).astype(jnp.bfloat16), scaled, inverse


def norm_backward(grad, scaled, inverse, gain):
    inner = grad * gain
    back = inverse * (
        inner
        - jnp.mean(inner, axis=-1, keepdims=True)
        - scaled * jnp.mean(inner * scaled, axis=-1, keepdims=True)
    )
    return back, jnp.sum(grad * scaled, axis=0, keepdims=True), jnp.sum(grad, axis=0, keepdims=True)


def per_device(groups_dp, shards, *arguments):
    (
        patches, embedding, first_gain, first_shift, joint_weight, output_weight,
        second_gain, second_shift, up_weight, up_bias, down_weight, down_bias,
        block_number, cotangent,
    ) = arguments
    f32, bf16 = jnp.float32, jnp.bfloat16
    _, rows, width_in = patches.shape
    model = output_weight.shape[1]
    half = model // 2
    unit = model // shards
    hidden_units = up_weight.shape[1]
    piece = hidden_units // (GROUPS * shards)
    embed_rows = embedding.shape[0]
    width = shards // GROUPS
    feature = model // GROUPS
    fast = groups_dp == 4 and shards == 8
    dp, seq = lax.axis_index("dp"), lax.axis_index("seq")
    own_group, own_part = seq // width, seq % width
    core = dp % 2 if fast else jnp.int32(0)
    chip = dp // 2 if fast else jnp.int32(0)

    everyone = [(d, s) for d in range(groups_dp) for s in range(shards)]

    def moved(value, rule):
        pairs = []
        for d, s in everyone:
            there = rule(d, s)
            pairs.append((d * shards + s, there[0] * shards + there[1]))
        return lax.ppermute(value, AXES, pairs)

    def along_groups(value, by):
        return moved(value, lambda d, s: (d, ((s // width + by) % GROUPS) * width + s % width))

    def along_parts(value, by):
        return moved(value, lambda d, s: (d, (s // width) * width + (s % width + by) % width))

    def to_core(value):
        return moved(value, lambda d, s: (d ^ 1, s))

    def to_chip(value):
        return moved(value, lambda d, s: (d ^ 2, s))

    def at_index(value, at):
        return lax.dynamic_index_in_dim(value, at, 0, keepdims=False)

    def after(value, *others):
        return lax.optimization_barrier((value, *others))[0]

    def gathered(quarters):
        if fast:
            mine = at_index(quarters, dp)
            whole = lax.all_gather(mine, AXES, axis=0, tiled=False)
            return whole.reshape(GROUPS, shards, *mine.shape)
        whole = lax.all_gather(quarters, "seq", axis=0, tiled=False)
        return jnp.swapaxes(whole, 0, 1)

    joint_quarters = jnp.transpose(joint_weight.reshape(unit, 3, GROUPS, feature), (2, 0, 1, 3)).reshape(
        GROUPS, unit, 3 * feature
    )
    embed_quarters = jnp.transpose(
        embedding.reshape(2, embed_rows // 2, 2, half), (0, 2, 1, 3)
    ).reshape(GROUPS, embed_rows // 2, half)
    last = joint_quarters[:, :, half:].reshape(GROUPS, 2, unit // 2, feature)
    pieces = gathered(
        jnp.concatenate(
            [embed_quarters, joint_quarters[:, :, :half], jnp.concatenate([last[:, 0], last[:, 1]], axis=-1)],
            axis=1,
        )
    )
    up_quarters = jnp.transpose(
        up_weight.reshape(unit, shards, GROUPS, piece), (2, 0, 1, 3)
    ).reshape(GROUPS, unit, model)
    later_in = jnp.concatenate(
        [
            up_quarters,
            down_weight.reshape(GROUPS, piece, model),
            output_weight.reshape(GROUPS, unit // GROUPS, model),
        ],
        axis=1,
    )
    later = gathered(after(later_in, pieces))
    output_full = jnp.swapaxes(later[:, :, 2 * unit :], 0, 1).reshape(GROUPS, feature, model)

    vectors = jnp.concatenate([first_gain, first_shift, second_gain, second_shift, down_bias, up_bias])
    count = vectors.shape[0]
    if fast:
        spread = jnp.where(jnp.arange(shards)[:, None] == seq, vectors[None], jnp.zeros((), bf16))
        for bit in (1, 2, 4):
            spread = spread + moved(spread, lambda d, s, bit=bit: (d, s ^ bit))
    else:
        spread = lax.all_gather(vectors, "seq", axis=0, tiled=False)
    vector_all = spread.astype(f32)
    gain_one, shift_one, gain_two, shift_two, bias_down = (
        vector_all[:, at * unit : (at + 1) * unit].reshape(1, model) for at in range(5)
    )
    bias_up = jnp.transpose(
        vector_all[:, 5 * unit :].reshape(shards, GROUPS, piece), (1, 0, 2)
    ).reshape(GROUPS, 1, model)

    ids = block_number[0]
    ends = jnp.sum((ids[None, :] <= ids[:, None]).astype(jnp.int32), axis=1)
    ends = ends.reshape(shards, 1, rows)
    place = jnp.concatenate([jnp.stack([own_group, own_part]).astype(jnp.int32), ends[:, 0, -1]])
    spot = jnp.stack([own_group, own_part, core]).astype(jnp.int32)

    flat_in = patches[0]
    tangent = cotangent[0]
    hidden, normed1, joint_full, *joint = embed(after(spot, ends), flat_in, pieces, gain_one, shift_one, unit)

    def back_home(parts):
        return [parts[0]] + [along_groups(parts[by], GROUPS - by) for by in range(1, GROUPS)]

    arrived = [
        [joint[head]] + [along_groups(joint[by * PER + head], by) for by in range(1, GROUPS)] for head in range(PER)
    ]
    others, outs, logs, home = [], [], [], []

    def exchange(head):
        packed = pack(arrived[head])
        others.append([along_parts(packed, by) for by in range(1, width)])

    exchange(0)
    exchange(1)
    for head in range(PER):
        *out, log = attention_forward(place, ends, arrived[head], others[head])
        outs.append(out)
        logs.append(log)
        home.append(back_home(out))
        if head + 2 < PER:
            arrived[head + 2][0] = after(arrived[head + 2][0], log)
            exchange(head + 2)
    resid, normed2, attended = whole_call(
        resid_kernel, "resid", 6, spot,
        [hidden, output_full, gain_two, shift_two] + [home[head][by] for by in range(GROUPS) for head in range(PER)],
        [((rows, model), f32), ((rows, model), bf16), ((GROUPS, feature, rows), bf16)],
    )
    attended = attended.reshape(model, rows)
    order = jnp.stack(
        [(1 - chip) * 2 + 1 - core, chip * 2 + 1 - core, (1 - chip) * 2 + core, chip * 2 + core]
    ).astype(jnp.int32)
    lowered, normed2_grad, given, kept_far, kept_near, bias_up_grad = mlp(order, normed2, tangent, later, bias_up)
    block_output, resid_grad, mixed_grad, sums_two, *grads_out = whole_call(
        mixed_kernel, "mixed", 8, spot,
        [resid, lowered, bias_down, normed2_grad, tangent, gain_two, shift_two, output_full],
        [((rows, model), bf16), ((rows, model), f32), ((rows, model), bf16), ((3, model), f32)]
        + [((HEAD_DIM, rows), bf16)] * (GROUPS * PER),
    )

    def added(*terms):
        total = terms[0].astype(f32)
        for term in terms[1:]:
            total = total + term.astype(f32)
        return total.astype(bf16)

    def pick(value, at, axis):
        return lax.dynamic_index_in_dim(value, at, axis, keepdims=False)

    def slow(value):
        return lax.psum(lax.psum_scatter(value, "seq", scatter_dimension=0, tiled=False), "dp")

    def over_groups(value, *marks):
        sends = [pick(value, (own_group + by) % GROUPS, 0) for by in range(1, GROUPS)]
        sends = [after(send, *marks) if marks else send for send in sends]
        return added(pick(value, own_group, 0), *[along_groups(send, by) for by, send in enumerate(sends, 1)])

    def sent_grads(head):
        return [grads_out[head]] + [along_groups(grads_out[by * PER + head], by) for by in range(1, GROUPS)]

    def finish(head):
        near, fars = unfinished[head]
        merged = merge(near, [along_parts(far, width - by) for by, far in enumerate(fars, 1)])
        joint_parts.append(back_home(merged))
        return merged

    def attend_back(head, *marks):
        grads = list(grads_in[head])
        if marks:
            grads[0] = after(grads[0], *marks)
        near, *fars = attention_backward(place, ends, logs[head], arrived[head], others[head], outs[head], grads)
        unfinished.append((near, fars))
        return near

    grads_in = [sent_grads(head) for head in range(PER)]
    unfinished, joint_parts = [], []
    if fast:
        kept = [kept_far, kept_near]
        swapped = to_core(given)

        def rows_of(value, low, turn=None):
            part = value[:, :unit] if low else value[:, unit:]
            return part if turn is None else pick(part.reshape(GROUPS, width, unit, model), turn, 1)

        first_out = added(rows_of(kept[0], True), rows_of(swapped[0], True))
        second_out = jnp.stack(
            [added(rows_of(kept[q], False, 1 - own_part), rows_of(swapped[q], False, 1 - own_part)) for q in range(2)]
        )
        from_chip, from_part = to_chip(first_out), along_parts(second_out, 1)
        mark = attend_back(0, first_out, second_out)
        from_chip, from_part = after(from_chip, mark), after(from_part, mark)
        first = added(rows_of(kept[1], True), rows_of(swapped[1], True), from_chip)
        first = first.reshape(GROUPS, width, unit, model)
        first_out = pick(first, 1 - own_part, 1)
        second = [
            added(rows_of(kept[q], False, own_part), rows_of(swapped[q], False, own_part), from_part[q])
            for q in range(2)
        ]
        from_part, from_chip = along_parts(first_out, 1), to_chip(second[0])
        mark = attend_back(1, first_out, second[0])
        from_chip, from_part = after(from_chip, mark), after(from_part, mark)
        both = jnp.stack([added(pick(first, own_part, 1), from_part), added(second[1], from_chip)], axis=1)
        merged = finish(0)
        group_own = over_groups(both).reshape(2 * unit, model)
        attend_back(2, both, merged[0])
    else:
        attend_back(0)
        attend_back(1)
        attend_back(2, finish(0)[0])
    finish(1)
    finish(2)
    joint_grad, hidden_grad, given_turned, kept_turned, sums_one = whole_call(
        hidden_kernel, "hidden_grad", 10, spot,
        [joint_full, hidden, gain_one, shift_one, resid_grad]
        + [joint_parts[head][by] for by in range(GROUPS) for head in range(PER)],
        [
            ((GROUPS, 3 * feature, rows), bf16), ((rows, model), bf16),
            ((half, rows), bf16), ((half, rows), bf16), ((2, model), f32),
        ],
    )

    def square(side):
        return whole_call(
            square_kernel, "square_gradient", 4, jnp.reshape(side, (1,)).astype(jnp.int32),
            [normed1, joint_grad, attended, mixed_grad], [((shards, 4, unit, half), bf16)],
        )[0]

    def phase_one(given, kept):
        shape = (GROUPS, width, 2, 2, *kept.shape[2:])
        terms = [kept.reshape(shape), to_core(given).reshape(shape)]
        return terms, (
            added(*[pick(term[:, :, 0], 1 - chip, 2) for term in terms]),
            added(*[pick(term[:, :, 1], 1 - own_part, 1) for term in terms]),
        )

    def phase_two(terms, sends, *marks):
        from_chip, from_part = to_chip(sends[0]), along_parts(sends[1], 1)
        if marks:
            from_chip, from_part = after(from_chip, *marks), after(from_part, *marks)
        first = added(*[pick(term[:, :, 0], chip, 2) for term in terms], from_chip)
        second = added(*[pick(term[:, :, 1], own_part, 1) for term in terms], from_part)
        outs_first, outs_second = pick(first, 1 - own_part, 1), pick(second, 1 - chip, 1)
        return (first, second), (outs_first, outs_second)

    def phase_three(state, sends, *marks):
        from_part, from_chip = along_parts(sends[0], 1), to_chip(sends[1])
        if marks:
            from_chip, from_part = after(from_chip, *marks), after(from_part, *marks)
        first, second = state
        return jnp.stack(
            [added(pick(first, own_part, 1), from_part), added(pick(second, chip, 1), from_chip)], axis=1
        )

    def phase_last(both, *marks):
        mine = over_groups(both, *marks)
        theirs = to_chip(mine)
        whole = jnp.stack([jnp.where(chip == 0, mine, theirs), jnp.where(chip == 0, theirs, mine)], axis=1)
        whole = whole.reshape(4, *whole.shape[2:])
        other = to_core(whole)
        return jnp.where(core == 0, whole, other).astype(f32), jnp.where(core == 0, other, whole).astype(f32)

    turned_shape = (shards, 4, half // 4, embed_rows)
    square_given, square_kept = square(1 - core), square(core)
    if fast:
        square_terms, square_sends = phase_one(square_given, square_kept)
        embed_given = embed_gradient(flat_in, after(given_turned, square_kept), shards)
        embed_kept = embed_gradient(flat_in, after(kept_turned, embed_given, *square_sends), shards)
        embed_terms, embed_sends = phase_one(embed_given.reshape(turned_shape), embed_kept.reshape(turned_shape))
        square_state, square_sends = phase_two(square_terms, square_sends, *embed_sends)
        patches_grad = patch_gradient(after(hidden_grad, *square_sends), pieces, width_in)[None]
        embed_state, embed_sends = phase_two(embed_terms, embed_sends, patches_grad)
        square_both = phase_three(square_state, square_sends, *embed_sends)
        square_halves = phase_last(square_both)
        embed_both = phase_three(embed_state, embed_sends, square_both)
        embed_halves = phase_last(embed_both)
        late = embed_both
        group_far = to_chip(group_own)
        pair_own = jnp.stack([group_own, group_far])
        pair_other = to_core(pair_own)
        mlp_shard = jnp.zeros((GROUPS, *group_own.shape), bf16)
        for at, value in ((3, pair_own[0]), (2, pair_own[1]), (1, pair_other[0]), (0, pair_other[1])):
            mlp_shard = lax.dynamic_update_index_in_dim(mlp_shard, value, order[at], 0)
    else:
        embed_given = embed_gradient(flat_in, given_turned, shards).reshape(turned_shape)
        embed_kept = embed_gradient(flat_in, kept_turned, shards).reshape(turned_shape)
        patches_grad = patch_gradient(hidden_grad, pieces, width_in)[None]
        square_halves = [slow(part).astype(f32) for part in (square_kept, square_given)]
        embed_halves = [slow(part).astype(f32) for part in (embed_kept, embed_given)]
        mlp_shard = jnp.stack([slow(kept_near), slow(given[1]), slow(kept_far), slow(given[0])])
    embed_shard = jnp.concatenate([got.reshape(half, embed_rows) for got in embed_halves], axis=0).T
    output_shard = jnp.concatenate([got[3] for got in square_halves], axis=-1)
    joint_shard = jnp.stack(
        [jnp.swapaxes(got[:3], 0, 1).reshape(unit, 2, 3, feature) for got in square_halves], axis=1
    ).reshape(unit, GROUPS, 3, feature)
    joint_shard = jnp.swapaxes(joint_shard, 1, 2).reshape(unit, 3 * model)
    mlp_shard = mlp_shard.astype(f32)
    up_grad = jnp.transpose(
        mlp_shard[:, :unit].reshape(GROUPS, unit, shards, piece), (1, 2, 0, 3)
    ).reshape(unit, hidden_units)
    down_grad = mlp_shard[:, unit:].reshape(GROUPS * piece, model)

    bias_up_natural = jnp.transpose(bias_up_grad.reshape(GROUPS, shards, piece), (1, 0, 2))
    packed = jnp.concatenate(
        [
            part.reshape(shards, -1)
            for part in (sums_one[0], sums_one[1], sums_two[0], sums_two[1], sums_two[2], bias_up_natural)
        ],
        axis=1,
    )
    if fast:
        packed = after(packed, late)
        packed = packed + to_core(packed)
        packed = packed + to_chip(packed)
        for bit in (1, 2, 4):
            packed = packed + moved(packed, lambda d, s, bit=bit: (d, s ^ bit))
    else:
        packed = lax.psum(packed, AXES)
    own_vectors = at_index(packed, seq)
    own = [own_vectors[at * unit : (at + 1) * unit] for at in range(5)]
    return (
        block_output[None],
        patches_grad,
        embed_shard,
        own[0],
        own[1],
        joint_shard,
        output_shard,
        own[2],
        own[3],
        up_grad,
        own_vectors[5 * unit :],
        down_grad,
        own[4],
    )


def solution(mesh):
    rows, columns, vector = P("dp", "seq", None), P("seq", None), P("seq")
    placed = (
        rows, columns, vector, vector, columns, columns, vector, vector,
        columns, vector, columns, vector, P("dp", None), rows,
    )
    given = (
        rows, rows, columns, vector, vector, columns, columns,
        vector, vector, columns, vector, columns, vector,
    )
    return jax.shard_map(
        functools.partial(per_device, mesh.shape["dp"], mesh.shape["seq"]),
        mesh=mesh,
        in_specs=placed,
        out_specs=given,
        check_vma=False,
    )
```
